32 devices in a mesh: col: 4 (over y, x), row: 8 (over z, core).
Axes of the slice: x: 2, y: 2, z: 4, core: 2. Of those that a mesh axis runs over, the one named last changes fastest.
Arguments:
- snapshots: bfloat16 [8192, 4096], P('row', 'col'), may hold values from -54 to 54
- rotations: bfloat16 [2, 4096, 1024], P(None, 'col'), may hold values from -1 to 2
Outputs:
- gram_first: float32 [4096, 1024], P(('col', 'row'))
- gram_second: float32 [4096, 1024], P(('col', 'row'))
- shrunk: bfloat16 [8192, 4096], P('row', 'col')
The draws below stay inside these ranges and needn't reach their ends.
All inputs are finite; a program needn't handle non-finite values.
Results may differ from the reference program's by a relative error of at most 0.012.
Values may be sent and summed in bfloat16 or wider, within the bound.
A program may use at most 64 MiB of HBM per device.

```python
import math
import jax
import jax.numpy as jnp
from jax import lax

BW = 512
ROWS_DEV = 1024
ROWS = 8192
COLS = 4096
N_COL = 4


def draw_snapshots(key, part):
    keys = jax.random.split(key, 6)
    positions = jnp.arange(ROWS, dtype=jnp.float32)
    width_rows = 1.2 * ROWS_DEV
    centres = jax.random.uniform(keys[5], (1, COLS), jnp.float32, 0.0, float(ROWS))
    offsets = (positions[:, None] - centres) / width_rows
    envelope = jnp.exp(-offsets * offsets) + 0.1
    mean_square = (width_rows * math.sqrt(math.pi / 2.0) + 0.2 * width_rows * math.sqrt(math.pi)) / ROWS + 0.01
    envelope = envelope / math.sqrt(mean_square)
    rough_rows = jax.random.uniform(keys[1], (ROWS, 1), jnp.float32, 0.75, 1.25)
    col_scale = jnp.exp(jax.random.uniform(keys[2], (1, COLS), jnp.float32, math.log(0.4), math.log(4.0)))
    values = jnp.clip(jax.random.normal(keys[0], (ROWS, COLS), jnp.float32), -4.0, 4.0)
    return jnp.clip(values * envelope * rough_rows * col_scale, -54.0, 54.0).astype(jnp.bfloat16)


def draw_rotations(key, part):
    width_pair = 2 * BW
    row_pos = jnp.arange(COLS) % width_pair
    identity = (row_pos[:, None] == jnp.arange(width_pair)[None, :]).astype(jnp.float32)
    noise = jnp.clip(jax.random.normal(key, (2, COLS, width_pair), jnp.float32), -4.0, 4.0)
    return (identity[None] + noise * (0.6 / math.sqrt(width_pair))).astype(jnp.bfloat16)


def setup_inputs(seed: int = 0) -> dict:
    seeds = jax.random.split(jax.random.key(seed), 3)
    snapshots = draw_snapshots(jax.random.fold_in(seeds[2], 71), 0)
    rotations = draw_rotations(jax.random.fold_in(seeds[2], 71), 0)
    return {"snapshots": snapshots, "rotations": rotations}


def gram_of(pair_cols):
    return lax.dot_general(pair_cols, pair_cols, (((0,), (0,)), ((), ())), preferred_element_type=jnp.float32) / ROWS

def first_step(inputs):
    pair_cols, rotation = inputs
    turned = jnp.dot(pair_cols, rotation, preferred_element_type=jnp.float32).astype(jnp.bfloat16)
    return (gram_of(pair_cols), turned)

def second_step(inputs):
    pair_cols, rotation = inputs
    moved = jnp.dot(pair_cols, rotation, preferred_element_type=jnp.float32)
    singular = jnp.sqrt(lax.optimization_barrier(jnp.sum(moved * moved, axis=0)) / ROWS + 1e-06)
    factor = jnp.maximum(singular - 1.8, 0.0) / singular
    return (gram_of(pair_cols), (moved * factor).astype(jnp.bfloat16))

def reference(snapshots, rotations):
    pairs = jnp.transpose(snapshots.reshape(ROWS, N_COL, 2 * BW), (1, 0, 2))
    rot_first = rotations[0].reshape(N_COL, 2 * BW, 2 * BW)
    rot_second = rotations[1].reshape(N_COL, 2 * BW, 2 * BW)
    gram_first, turned = lax.map(first_step, (pairs, rot_first))
    left_blocks = jnp.roll(turned[:, :, :BW], 1, axis=0)
    second_pairs = jnp.concatenate([left_blocks, turned[:, :, BW:]], axis=2)
    gram_second, shrunk = lax.map(second_step, (second_pairs, rot_second))
    return (gram_first.reshape(N_COL * 2 * BW, 2 * BW), gram_second.reshape(N_COL * 2 * BW, 2 * BW), jnp.transpose(shrunk, (1, 0, 2)).reshape(ROWS, N_COL * 2 * BW))
```

```python
import functools

import jax
import jax.numpy as jnp
from jax import lax
from jax.experimental import pallas as pl
from jax.experimental.pallas import tpu as pltpu
from jax.sharding import PartitionSpec as P

TILE = 256
LANE = 128

UNITS = ((0, 0), (0, 2), (0, 3), (0, 1), (2, 2), (2, 3), (2, 1), (3, 3), (3, 1), (1, 1))
FIRST = (0, 1, 2, 3, 4, 5, 6, 7, 8, 9)
STAGES = ((4, 5, 7), (0, 1, 2), (8, 3, 6, 9))


def kernel(
    n, n_col, x_hbm, rot_hbm, g1_hbm, g2_hbm, out_hbm,
    x, rot, left, pair, moved, part, peer, sums, landed, turn_out, turn_in,
    gram_out, energy, energy_in, shrunk,
    flipped, load_sem, left_send, left_recv, core_send, core_recv, z_send, z_recv,
    turn_send, turn_recv, e_send, e_recv, store_sem, shrunk_sem,
):
    rows, width = x.shape
    half = width // 2
    block = width // n
    groups = n // 2
    symmetric = n == 8 and block == LANE
    total_rows = rows * n
    tiles = width // TILE
    row_tiles = rows // TILE
    per_tile = TILE // (2 * block)

    me_col = lax.axis_index("col")
    me = lax.axis_index("row")
    core = lax.rem(me, 2)
    group = lax.div(me, 2)
    partner = me + 1 - 2 * core

    def peer_at(step):
        return lax.rem(me + step, n)

    load_x = pltpu.make_async_copy(x_hbm, x, load_sem.at[0])
    load_r0 = [
        pltpu.make_async_copy(
            rot_hbm.at[0, :, pl.ds(h * half, half)], rot.at[0, :, pl.ds(h * half, half)],
            load_sem.at[1 + h],
        )
        for h in range(2)
    ]
    load_r1 = pltpu.make_async_copy(rot_hbm.at[1], rot.at[1], load_sem.at[3])
    load_x.start()
    load_r0[0].start()
    load_r0[1].start()
    load_r1.start()

    following = lax.rem(me_col + 1, n_col)
    preceding = lax.rem(me_col + n_col - 1, n_col)
    barrier = pltpu.get_barrier_semaphore()
    for other in (following, preceding):
        pl.semaphore_signal(
            barrier, inc=1, device_id={"col": other, "row": me},
            device_id_type=pl.DeviceIdType.MESH,
        )
    for step in range(1, n):
        pl.semaphore_signal(
            barrier, inc=1, device_id={"col": me_col, "row": peer_at(step)},
            device_id_type=pl.DeviceIdType.MESH,
        )

    def remote(src, dst, send_sem, recv_sem, col, row):
        return pltpu.make_async_remote_copy(
            src_ref=src, dst_ref=dst, send_sem=send_sem, recv_sem=recv_sem,
            device_id={"col": col, "row": row}, device_id_type=pl.DeviceIdType.MESH,
        )

    def turn(into, first, column):
        def body(t, _):
            span = pl.ds(pl.multiple_of(t * TILE, TILE), TILE)
            into[span, pl.ds(column - first, TILE)] = jnp.dot(
                x[span, :], rot[0, :, pl.ds(column, TILE)], preferred_element_type=jnp.float32
            ).astype(jnp.bfloat16)
            return 0
        lax.fori_loop(0, row_tiles, body, 0)

    pieces = half // TILE
    left_copy = [
        remote(
            left.at[:, pl.ds(h * TILE, TILE)], pair.at[:, pl.ds(h * TILE, TILE)],
            left_send.at[h], left_recv.at[h], following, me,
        )
        for h in range(pieces)
    ]
    load_x.wait()
    load_r0[0].wait()
    turn(left, 0, 0)
    pl.semaphore_wait(barrier, n + 1)
    left_copy[0].start()

    def owned(u):
        g = UNITS[u][0]
        return [v for v in range(len(UNITS)) if UNITS[v][0] == g].index(u)

    def core_copy(s, u):
        return remote(
            part.at[s, 1 - core, u], peer.at[s, u],
            core_send.at[s, u], core_recv.at[s, u], me_col, partner,
        )

    def z_copy(s, u):
        g = UNITS[u][0] if symmetric else lax.rem(group + u, groups)
        k = lax.rem(g - group + 2 * groups - 1, groups)
        if symmetric:
            v = owned(u)
            return remote(
                sums.at[s, u], landed.at[s, v, k], z_send.at[s, u], z_recv.at[s, v, k],
                me_col, 2 * g + core,
            )
        return remote(
            sums.at[s, g], landed.at[s, 0, k], z_send.at[s, k], z_recv.at[s, 0, k],
            me_col, 2 * g + core,
        )

    def added(s, u):
        return part[s, core, u].astype(jnp.float32) + peer[s, u].astype(jnp.float32)

    def turn_copy(s, u, e):
        g, c = UNITS[u]
        return remote(
            turn_out.at[s, owned(u), e], turn_in.at[s, g, core],
            turn_send.at[s, owned(u), e], turn_recv.at[s, g, core], me_col, 2 * c + e,
        )

    def flip(source, g):
        flipped[g] = source[:, g * TILE:(g + 1) * TILE].T

    def pair_terms(s, source, units):
        for u in units:
            g, c = UNITS[u]
            term = jnp.dot(
                flipped[g], source[:, c * TILE:(c + 1) * TILE],
                preferred_element_type=jnp.float32,
            ).astype(jnp.bfloat16)
            part[s, 0, u] = term[:LANE]
            part[s, 1, u] = term[LANE:]
            core_copy(s, u).start()

    def pair_pass(s, units):
        for u in units:
            core_copy(s, u).wait_recv()

            @pl.when(group != UNITS[u][0])
            def _():
                sums[s, u] = added(s, u).astype(jnp.bfloat16)
                z_copy(s, u).start()

    def pair_sum(s, units):
        for u in units:
            g, c = UNITS[u]

            @pl.when(group == g)
            def _():
                v = owned(u)
                total = added(s, u)
                for k in range(groups - 1):
                    remote(
                        sums.at[s, u], landed.at[s, v, k], z_send.at[s, u], z_recv.at[s, v, k],
                        me_col, partner,
                    ).wait_recv()
                    total = total + landed[s, v, k].astype(jnp.float32)
                total = total / total_rows
                if c != g:
                    for e in range(2):
                        turn_out[s, v, e] = total[:, e * LANE:(e + 1) * LANE].T.astype(jnp.bfloat16)
                        turn_copy(s, u, e).start()
                gram_out[s, :, c * TILE:(c + 1) * TILE] = total

    def pair_turned(s, units):
        for u in units:
            g, c = UNITS[u]
            if c != g:

                @pl.when(group == c)
                def _():
                    for e in range(2):
                        remote(
                            turn_out.at[s, 0, 0], turn_in.at[s, g, e], turn_send.at[s, 0, 0],
                            turn_recv.at[s, g, e], me_col, partner,
                        ).wait_recv()
                        gram_out[s, :, (2 * g + e) * LANE:(2 * g + e + 1) * LANE] = turn_in[
                            s, g, e
                        ].astype(jnp.float32)

    def pair_drain(s, units):
        for u in units:
            g, c = UNITS[u]
            core_copy(s, u).wait_send()

            @pl.when(group != g)
            def _():
                z_copy(s, u).wait_send()

            if c != g:

                @pl.when(group == g)
                def _():
                    for e in range(2):
                        turn_copy(s, u, e).wait_send()

    def rows_copy(s, q):
        span = pl.ds(q * per_tile, per_tile)
        return remote(
            part.at[s, 1 - core, span], peer.at[s, span],
            core_send.at[s, q], core_recv.at[s, q], me_col, partner,
        )

    def rows_terms(s, source):
        def body(q, _):
            turned_tile = source[:, pl.ds(pl.multiple_of(q * TILE, TILE), TILE)].T
            for m in range(tiles):
                term = jnp.dot(
                    turned_tile, source[:, m * TILE:(m + 1) * TILE],
                    preferred_element_type=jnp.float32,
                ).astype(jnp.bfloat16)
                for e in range(2 * per_tile):
                    part[s, e % 2, q * per_tile + e // 2, :, m * TILE:(m + 1) * TILE] = term[
                        e * block:(e + 1) * block, :
                    ]
            rows_copy(s, q).start()
            return 0
        lax.fori_loop(0, tiles, body, 0)

    def rows_pass(s):
        for q in range(tiles):
            rows_copy(s, q).wait_recv()

        def body(k, _):
            g = lax.rem(group + k, groups)
            sums[s, g] = added(s, g).astype(jnp.bfloat16)
            z_copy(s, k).start()
            return 0
        lax.fori_loop(1, groups, body, 0)

    def rows_sum(s):
        total = added(s, group)
        for k in range(1, groups):
            z_copy(s, k).wait_recv()
            total = total + landed[s, 0, k - 1].astype(jnp.float32)
        gram_out[s] = total / total_rows

    def gram_store(s, target):
        return pltpu.make_async_copy(gram_out.at[s], target, store_sem.at[s])

    if symmetric:
        due = []
        for g in (0, 3, 2, 1):
            now = [u for u in FIRST if UNITS[u][0] == g]
            flip(x, g)
            pair_terms(0, x, now)
            pair_pass(0, due)
            due = now
    else:
        rows_terms(0, x)
    for h in range(1, pieces):
        turn(left, 0, h * TILE)
        left_copy[h].start()
    if symmetric:
        pair_pass(0, due)
    else:
        rows_pass(0)
    load_r0[1].wait()
    for h in range(pieces):
        turn(pair, 0, half + h * TILE)
    if symmetric:
        flip(pair, 2)
        flip(pair, 3)
        pair_terms(1, pair, STAGES[0])

    load_r1.wait()

    def add_moved(first, depth, fresh):
        def body(t, acc):
            span = pl.ds(pl.multiple_of(t * TILE, TILE), TILE)
            value = jnp.dot(
                pair[span, pl.ds(first, depth)], rot[1, pl.ds(first, depth), :],
                preferred_element_type=jnp.float32,
            )
            if not fresh:
                value = value + moved[span, :]
            moved[span, :] = value
            return acc + jnp.sum(value * value, axis=0, keepdims=True)
        return lax.fori_loop(0, row_tiles, body, jnp.zeros((1, width), jnp.float32))

    add_moved(half, half, True)
    if symmetric:
        pair_pass(1, STAGES[0])
    left_copy[0].wait_recv()
    if symmetric:
        flip(pair, 0)
        pair_terms(1, pair, STAGES[1])
        pair_pass(1, STAGES[1])
    for h in range(pieces - 1):
        if h > 0:
            left_copy[h].wait_recv()
        add_moved(h * TILE, TILE, False)
    if symmetric:
        pair_sum(0, FIRST)
        pair_turned(0, FIRST)
    else:
        rows_sum(0)
    gram_store(0, g1_hbm).start()
    if symmetric:
        pair_sum(1, STAGES[0])
    left_copy[pieces - 1].wait_recv()
    if symmetric:
        flip(pair, 1)
        pair_terms(1, pair, STAGES[2])
        pair_pass(1, STAGES[2])
    else:
        rows_terms(1, pair)
    energy[...] = add_moved(half - TILE, TILE, False)

    def e_copy(step):
        return remote(
            energy, energy_in.at[step - 1], e_send.at[step - 1], e_recv.at[step - 1],
            me_col, peer_at(step),
        )

    for step in range(1, n):
        e_copy(step).start()
    if symmetric:
        pair_sum(1, STAGES[1])
        pair_turned(1, STAGES[0] + STAGES[1])
    else:
        rows_pass(1)
    total = energy[...]
    for step in range(1, n):
        e_copy(step).wait_recv()
        total = total + energy_in[step - 1]
    singular = jnp.sqrt(total / total_rows + 1e-06)
    factor = jnp.maximum(singular - 1.8, 0.0) / singular

    def out_copy(t):
        span = pl.ds(pl.multiple_of(t * TILE, TILE), TILE)
        return pltpu.make_async_copy(shrunk.at[span, :], out_hbm.at[span, :], shrunk_sem.at[t])

    def shrink(t, _):
        span = pl.ds(pl.multiple_of(t * TILE, TILE), TILE)
        shrunk[span, :] = (moved[span, :] * factor).astype(jnp.bfloat16)
        out_copy(t).start()
        return 0

    lax.fori_loop(0, row_tiles, shrink, 0)
    if symmetric:
        pair_sum(1, STAGES[2])
        pair_turned(1, STAGES[2])
    else:
        rows_sum(1)
    gram_store(1, g2_hbm).start()

    for h in range(pieces):
        left_copy[h].wait_send()
    for s in range(2):
        if symmetric:
            pair_drain(s, FIRST)
        else:
            for q in range(tiles):
                rows_copy(s, q).wait_send()
            for k in range(1, groups):
                z_copy(s, k).wait_send()
    for step in range(1, n):
        e_copy(step).wait_send()
    for t in range(row_tiles):
        out_copy(t).wait()
    gram_store(0, g1_hbm).wait()
    gram_store(1, g2_hbm).wait()


def finish(*refs):
    sources, targets, sem = refs[:3], refs[3:6], refs[6]
    stores = [
        pltpu.make_async_copy(source, target, sem.at[at])
        for at, (source, target) in enumerate(zip(sources, targets))
    ]
    for store in stores:
        store.start()
    for store in stores:
        store.wait()


def per_device(n, n_col, snapshots, rotations):
    rows, width = snapshots.shape
    half = width // 2
    block = width // n
    groups = n // 2
    tiles = width // TILE
    symmetric = n == 8 and block == LANE
    units = len(UNITS) if symmetric else groups
    reach = TILE if symmetric else width
    owned = 4 if symmetric else 1
    sends = units if symmetric else max(groups - 1, tiles)
    bf16, f32, dma = jnp.bfloat16, jnp.float32, pltpu.SemaphoreType.DMA
    anywhere = pl.BlockSpec(memory_space=pl.ANY)
    shapes = (
        jax.ShapeDtypeStruct((block, width), f32),
        jax.ShapeDtypeStruct((block, width), f32),
        jax.ShapeDtypeStruct((rows, width), bf16),
    )
    results = pl.pallas_call(
        functools.partial(kernel, n, n_col),
        out_shape=tuple(pltpu.VMEM(shape.shape, shape.dtype) for shape in shapes),
        in_specs=[anywhere] * 2,
        out_specs=(anywhere,) * 3,
        scratch_shapes=[
            pltpu.VMEM((rows, width), bf16),
            pltpu.VMEM((2, width, width), bf16),
            pltpu.VMEM((rows, half), bf16),
            pltpu.VMEM((rows, width), bf16),
            pltpu.VMEM((rows, width), f32),
            pltpu.VMEM((2, 2, units, block, reach), bf16),
            pltpu.VMEM((2, units, block, reach), bf16),
            pltpu.VMEM((2, units, block, reach), bf16),
            pltpu.VMEM((2, owned, groups - 1, block, reach), bf16),
            pltpu.VMEM((2, 4, 2, LANE, LANE), bf16),
            pltpu.VMEM((2, 4, 2, LANE, LANE), bf16),
            pltpu.VMEM((2, block, width), f32),
            pltpu.VMEM((1, width), f32),
            pltpu.VMEM((n - 1, 1, width), f32),
            pltpu.VMEM((rows, width), bf16),
            pltpu.VMEM((tiles, TILE, rows), bf16),
            dma((4,)),
            dma((half // TILE,)),
            dma((half // TILE,)),
            dma((2, sends)),
            dma((2, sends)),
            dma((2, sends)),
            dma((2, owned, groups - 1)),
            dma((2, 4, 2)),
            dma((2, 4, 2)),
            dma((n - 1,)),
            dma((n - 1,)),
            dma((2,)),
            dma((rows // TILE,)),
        ],
        compiler_params=pltpu.CompilerParams(
            collective_id=0, has_side_effects=True, vmem_limit_bytes=44 * 1024 * 1024
        ),
    )(
        *(pltpu.with_memory_space_constraint(a, pltpu.HBM) for a in (snapshots, rotations))
    )
    return pl.pallas_call(
        finish,
        out_shape=shapes,
        in_specs=[anywhere] * 3,
        out_specs=(anywhere,) * 3,
        scratch_shapes=[dma((3,))],
    )(*(pltpu.with_memory_space_constraint(r, pltpu.VMEM) for r in results))


def solution(mesh):
    return jax.shard_map(
        functools.partial(per_device, mesh.shape["row"], mesh.shape["col"]),
        mesh=mesh,
        in_specs=(P("row", "col"), P(None, "col", None)),
        out_specs=(P(("col", "row"), None), P(("col", "row"), None), P("row", "col")),
        check_vma=False,
    )
```

```python
import functools

import jax
import jax.numpy as jnp
from jax import lax
from jax.experimental import pallas as pl
from jax.experimental.pallas import tpu as pltpu
from jax.sharding import PartitionSpec as P

TILE = 256
LANE = 128
CHUNKS = 4


def paired_kernel(
    n_col, x_hbm, rot_hbm, g1, g2, out,
    x, rot, left, pair, moved, flip_x, flip_p, strip,
    a_part, a_peer, a_sums, a_near, a_far, a_total, a_turn, a_turned,
    b_part, b_peer, b_sums, b_near, b_far, b_turn, b_turned,
    c_part, c_peer, c_sums, c_near, c_far, c_turn, c_turned,
    d_part, d_peer, d_sums, d_near, d_far, d_land, d_turn, d_turned,
    energy, energy_in,
    load_sem, left_send, left_recv, a_core, a_first, a_second, a_mirror,
    b_core, b_first, b_second, b_mirror,
    c_core, c_first, c_second, c_mirror_send, c_mirror_recv,
    d_core, d_first, d_second, d_z, d_mirror_send, d_mirror_recv, e_sem,
):
    n = 8
    rows, width = x.shape
    half = width // 2
    scale = 1.0 / (rows * n)
    chunk = rows // CHUNKS
    f32, bf16 = jnp.float32, jnp.bfloat16

    me_col = lax.axis_index("col")
    me = lax.axis_index("row")
    core = lax.rem(me, 2)
    z = lax.div(me, 2)
    partner = me + 1 - 2 * core
    beside = z + 1 - 2 * lax.rem(z, 2)
    across = 3 - z
    opposite = lax.rem(z + 2, 4)
    following = lax.rem(me_col + 1, n_col)
    preceding = lax.rem(me_col + n_col - 1, n_col)

    def rows_of(q):
        return pl.ds(q * chunk, chunk)

    def load(source, target, at):
        return pltpu.make_async_copy(source, target, load_sem.at[at])

    load_x = [load(x_hbm.at[rows_of(q)], x.at[rows_of(q)], q) for q in range(CHUNKS)]
    parts = ((0, 0, TILE), (0, TILE, TILE), (0, half, half), (1, 0, width))
    load_r = [
        load(
            rot_hbm.at[s, :, pl.ds(first, size)], rot.at[s, :, pl.ds(first, size)], CHUNKS + k
        )
        for k, (s, first, size) in enumerate(parts)
    ]
    load_x[0].start()
    load_r[0].start()
    for q in range(1, CHUNKS):
        load_x[q].start()
    for k in range(1, 4):
        load_r[k].start()

    barrier = pltpu.get_barrier_semaphore()
    for other in (following, preceding):
        pl.semaphore_signal(
            barrier, inc=1, device_id={"col": other, "row": me},
            device_id_type=pl.DeviceIdType.MESH,
        )
    for step in range(1, n):
        pl.semaphore_signal(
            barrier, inc=1, device_id={"col": me_col, "row": lax.rem(me + step, n)},
            device_id_type=pl.DeviceIdType.MESH,
        )

    def remote(src, dst, send_sem, recv_sem, col, row):
        return pltpu.make_async_remote_copy(
            src_ref=src, dst_ref=dst, send_sem=send_sem, recv_sem=recv_sem,
            device_id={"col": col, "row": row}, device_id_type=pl.DeviceIdType.MESH,
        )

    def to_chip(src, dst, sems, at, chip):
        return remote(src, dst, sems.at[0, at], sems.at[1, at], me_col, 2 * chip + core)

    def mul(a, b):
        return jnp.dot(a, b, preferred_element_type=f32)

    def when(condition, run):
        if condition is True:
            run()
        else:
            pl.when(condition)(run)

    def left_copy(k):
        q = k % CHUNKS
        first, size = ((0, TILE), (TILE, LANE), (TILE + LANE, LANE))[k // CHUNKS]
        here = (rows_of(q), pl.ds(first, size))
        return remote(
            left.at[here], pair.at[here], left_send.at[k], left_recv.at[k], following, me
        )

    load_r[0].wait()
    for q in range(CHUNKS):
        load_x[q].wait()
        left[rows_of(q), 0:TILE] = mul(x[rows_of(q), :], rot[0, :, 0:TILE]).astype(bf16)
        if q == 0:
            pl.semaphore_wait(barrier, n + 1)
        left_copy(q).start()
    load_r[1].wait()
    for q in range(CHUNKS):
        left[rows_of(q), TILE:half] = mul(x[rows_of(q), :], rot[0, :, TILE:half]).astype(bf16)
        left_copy(CHUNKS + q).start()
    for q in range(CHUNKS):
        left_copy(2 * CHUNKS + q).start()

    def core_copy(part, peer, sems, at):
        return remote(
            part.at[1 - core, at], peer.at[at], sems.at[0, at], sems.at[1, at], me_col, partner
        )

    def added(part, peer, at, span):
        return part[core, at, span, :].astype(f32) + peer[at, span, :].astype(f32)

    class Fly:
        def __init__(self, part, peer, sums, near, far, near_sems, far_sems, base, span, first, second,
                     shift=0, live=lambda d: True):
            self.part, self.peer, self.sums, self.near, self.far = part, peer, sums, near, far
            self.near_sems, self.far_sems, self.base, self.span = near_sems, far_sems, base, span
            self.first, self.second, self.shift, self.live = first, second, shift, live

        def near_copy(self, slot, d):
            return to_chip(
                self.sums.at[d - self.shift, self.span], self.near.at[slot, self.span],
                self.near_sems, 2 * self.base + slot, self.first,
            )

        def far_copy(self):
            return to_chip(
                self.sums.at[self.second - self.shift, self.span], self.far.at[self.span],
                self.far_sems, self.base, self.second,
            )

        def term(self, d):
            return added(self.part, self.peer, d - self.shift, self.span)

        def send_near(self):
            for slot, d in enumerate((self.first, opposite)):
                def run(slot=slot, d=d):
                    self.sums[d - self.shift, self.span, :] = self.term(d).astype(bf16)
                    self.near_copy(slot, d).start()
                when(self.live(d), run)

        def send_far(self):
            def run():
                d = self.second
                self.near_copy(1, d).wait_recv()
                self.sums[d - self.shift, self.span, :] = (
                    self.term(d) + self.near[1, self.span, :].astype(f32)
                ).astype(bf16)
                self.far_copy().start()
            when(self.live(self.second), run)

        def total(self):
            self.near_copy(0, z).wait_recv()
            to_chip(
                self.sums.at[z - self.shift, self.span], self.far.at[self.span],
                self.far_sems, self.base, self.second,
            ).wait_recv()
            return (
                self.term(z) + self.near[0, self.span, :].astype(f32)
                + self.far[self.span, :].astype(f32)
            ) * scale

        def drain(self):
            for slot, d in enumerate((self.first, opposite)):
                when(self.live(d), lambda slot=slot, d=d: self.near_copy(slot, d).wait_send())
            when(self.live(self.second), lambda: self.far_copy().wait_send())

    everything = pl.ds(0, LANE)
    upper, lower = pl.ds(0, LANE // 2), pl.ds(LANE // 2, LANE // 2)
    a_sum = (
        Fly(a_part, a_peer, a_sums, a_near, a_far, a_first, a_second, 0, upper, beside, across),
        Fly(a_part, a_peer, a_sums, a_near, a_far, a_first, a_second, 1, lower, beside, across),
    )
    b_sum = Fly(
        b_part, b_peer, b_sums, b_near, b_far, b_first, b_second, 0, everything, beside, across,
        shift=2, live=lambda d: d >= 2,
    )

    class Direct:
        def __init__(self, part, peer, sums, land, sems):
            self.part, self.peer, self.sums, self.land, self.sems = part, peer, sums, land, sems

        def copy(self, k, d):
            return to_chip(self.sums.at[d], self.land.at[k - 1], self.sems, k - 1, d)

        def send(self):
            for k in (2, 1, 3):
                d = lax.rem(z + k, 4)
                self.sums[d] = added(self.part, self.peer, d, everything).astype(bf16)
                self.copy(k, d).start()

        def total(self):
            value = added(self.part, self.peer, z, everything)
            for k in (1, 3, 2):
                to_chip(
                    self.sums.at[z], self.land.at[k - 1], self.sems, k - 1, lax.rem(z + k, 4)
                ).wait_recv()
                value = value + self.land[k - 1].astype(f32)
            return value * scale

        def drain(self):
            for k in (1, 2, 3):
                self.copy(k, lax.rem(z + k, 4)).wait_send()

    c_sum = Fly(
        c_part, c_peer, c_sums, c_near, c_far, c_first, c_second, 0, everything, beside, across,
        live=lambda d: d != 1,
    )
    d_sum = (
        Fly(
            d_part.at[0], d_peer.at[0], d_sums.at[0], d_near, d_far, d_first, d_second, 0,
            everything, beside, across,
        ),
        Direct(d_part.at[1], d_peer.at[1], d_sums.at[1], d_land, d_z),
    )

    def column(block):
        if isinstance(block, int):
            return pl.ds(block * LANE, LANE)
        return pl.ds(pl.multiple_of(block * LANE, LANE), LANE)

    for d in range(4):
        flip_x[d] = x[:, d * TILE:(d + 1) * TILE].T
        for k in range(3):
            m = (d + k) % 4
            term = mul(flip_x[d], x[:, m * TILE:(m + 1) * TILE]).astype(bf16)
            for e in range(2):
                for b in range(2):
                    slot = 2 * k + b - e
                    if 0 <= slot <= 4:
                        a_part[e, d, :, slot * LANE:(slot + 1) * LANE] = term[
                            e * LANE:(e + 1) * LANE, b * LANE:(b + 1) * LANE
                        ]
        core_copy(a_part, a_peer, a_core, d).start()

    load_r[2].wait()

    def turn_right(first):
        def body(t, _):
            span = pl.ds(pl.multiple_of(t * TILE, TILE), TILE)
            pair[span, first:first + TILE] = mul(
                x[span, :], rot[0, :, first:first + TILE]
            ).astype(bf16)
            return 0
        lax.fori_loop(0, rows // TILE, body, 0)

    turn_right(half)
    for d in range(4):
        core_copy(a_part, a_peer, a_core, d).wait_recv()
    for fly in a_sum:
        fly.send_near()
    turn_right(half + TILE)

    for d in (2, 3):
        flip_p[d * TILE:(d + 1) * TILE, :] = pair[:, d * TILE:(d + 1) * TILE].T
        term = mul(flip_p[d * TILE:(d + 1) * TILE, :], pair[:, half:]).astype(bf16)
        for e in range(2):
            for k in range(3):
                at = (2 * (d - 2) + e + k) % 4 * LANE
                b_part[e, d - 2, :, k * LANE:(k + 1) * LANE] = term[
                    e * LANE:(e + 1) * LANE, at:at + LANE
                ]
        core_copy(b_part, b_peer, b_core, d - 2).start()

    load_r[3].wait()

    def move_right(t, _):
        span = pl.ds(pl.multiple_of(t * TILE, TILE), TILE)
        moved[span, :] = mul(pair[span, half:], rot[1, half:, :])
        return 0

    lax.fori_loop(0, rows // TILE, move_right, 0)
    for d in range(2):
        core_copy(b_part, b_peer, b_core, d).wait_recv()
    b_sum.send_near()
    a_sum[0].send_far()

    for q in range(CHUNKS):
        left_copy(q).wait_recv()
        flip_p[0:TILE, q * chunk:(q + 1) * chunk] = pair[rows_of(q), 0:TILE].T
    for d in (2, 3, 0):
        term = mul(flip_p[d * TILE:(d + 1) * TILE, :], pair[:, 0:TILE]).astype(bf16)
        c_part[0, d] = term[:LANE]
        c_part[1, d] = term[LANE:]
        core_copy(c_part, c_peer, c_core, d).start()
    a_sum[1].send_far()

    def move_left(t, _):
        span = pl.ds(pl.multiple_of(t * TILE, TILE), TILE)
        moved[span, :] += mul(pair[span, 0:TILE], rot[1, 0:TILE, :])
        return 0

    lax.fori_loop(0, rows // TILE, move_left, 0)
    for d in (2, 3, 0):
        core_copy(c_part, c_peer, c_core, d).wait_recv()
    c_sum.send_near()
    b_sum.send_far()

    for q in range(CHUNKS):
        left_copy(CHUNKS + q).wait_recv()
        flip_p[TILE:TILE + LANE, q * chunk:(q + 1) * chunk] = pair[rows_of(q), column(2)].T
    term = mul(flip_p[0:TILE + LANE, :], pair[:, column(2)]).astype(bf16)
    for i in range(4):
        at = min(i, 2) * LANE
        d_part[0, i % 2, i // 2] = term[at:at + LANE]
    for d in range(2):
        core_copy(d_part.at[0], d_peer.at[0], d_core.at[0], d).start()
    term = mul(flip_p[half:, :], pair[:, column(2)]).astype(bf16)
    for i in range(4):
        d_part[0, i % 2, 2 + i // 2] = term[i * LANE:(i + 1) * LANE]
    for d in range(2, 4):
        core_copy(d_part.at[0], d_peer.at[0], d_core.at[0], d).start()

    def strip_rows(q):
        span = rows_of(q)
        left_copy(2 * CHUNKS + q).wait_recv()
        flip_p[TILE + LANE:half, q * chunk:(q + 1) * chunk] = pair[span, column(3)].T
        value = mul(flip_p[:, q * chunk:(q + 1) * chunk], pair[span, column(3)])
        if q > 0:
            value = value + strip[...]
        if q < CHUNKS - 1:
            strip[...] = value
        else:
            for i in range(n):
                d_part[1, i % 2, i // 2] = value[i * LANE:(i + 1) * LANE].astype(bf16)
            for d in range(4):
                core_copy(d_part.at[1], d_peer.at[1], d_core.at[1], d).start()

    def move_rows(q):
        span = rows_of(q)
        value = moved[span, :] + mul(pair[span, TILE:half], rot[1, TILE:half, :])
        moved[span, :] = value
        return jnp.sum(value * value, axis=0, keepdims=True)

    strip_rows(0)
    squares = move_rows(0)
    for d in range(4):
        core_copy(d_part.at[0], d_peer.at[0], d_core.at[0], d).wait_recv()
    d_sum[0].send_near()
    c_sum.send_far()
    for q in range(1, CHUNKS):
        strip_rows(q)
        squares = squares + move_rows(q)
    energy[...] = squares

    def e_copy(step):
        return remote(
            energy, energy_in.at[step - 1], e_sem.at[0, step - 1], e_sem.at[1, step - 1],
            me_col, lax.rem(me + step, n),
        )

    for step in range(1, n):
        e_copy(step).start()
    for d in range(4):
        core_copy(d_part.at[1], d_peer.at[1], d_core.at[1], d).wait_recv()
    d_sum[1].send()
    d_sum[0].send_far()

    def a_mirror_copy(k):
        return remote(
            a_turn.at[k - 1], a_turned.at[k - 1], a_mirror.at[0, k - 1], a_mirror.at[1, k - 1],
            me_col, lax.rem(me + k, n),
        )

    def b_mirror_copy():
        return remote(
            b_turn, b_turned, b_mirror.at[0], b_mirror.at[1], me_col, 4 + lax.rem(me + 1, 4)
        )

    def c_mirror_copy(m, slot):
        return remote(
            c_turn.at[m], c_turned.at[slot], c_mirror_send.at[m], c_mirror_recv.at[slot],
            me_col, m,
        )

    def d_mirror_copy(s, slot):
        return remote(
            d_turn.at[s], d_turned.at[s, slot], d_mirror_send.at[s], d_mirror_recv.at[s, slot],
            me_col, 2 + s,
        )

    for fly in a_sum:
        a_total[fly.span, :] = fly.total()
    for k in (3, 2, 1):
        a_turn[k - 1] = a_total[:, k * LANE:(k + 1) * LANE].T.astype(bf16)
        a_mirror_copy(k).start()
    for k in range(5):
        g1[:, column(lax.rem(me + k, n))] = a_total[:, k * LANE:(k + 1) * LANE]

    @pl.when(z >= 2)
    def _():
        value = b_sum.total()
        b_turn[...] = value[:, LANE:2 * LANE].T.astype(bf16)
        b_mirror_copy().start()
        for k in range(3):
            g2[:, column(4 + lax.rem(me + k, 4))] = value[:, k * LANE:(k + 1) * LANE]

    @pl.when(z != 1)
    def _():
        g2[:, 0:TILE] = c_sum.total()

    @pl.when(z >= 2)
    def _():
        for m in range(2):
            c_turn[m] = g2[:, m * LANE:(m + 1) * LANE].T.astype(bf16)
            c_mirror_copy(m, me - 4).start()

    total = energy[...]
    for step in range(1, n):
        e_copy(step).wait_recv()
        total = total + energy_in[step - 1]
    singular = jnp.sqrt(total * scale + 1e-06)
    factor = jnp.maximum(singular - 1.8, 0.0) / singular

    def shrink(t, _):
        span = pl.ds(pl.multiple_of(t * TILE, TILE), TILE)
        out[span, :] = (moved[span, :] * factor).astype(bf16)
        return 0

    lax.fori_loop(0, rows // TILE, shrink, 0)

    def d_apart(s):
        return (me != 3) & (me != 2) if s == 0 else me != 3

    def d_finish(s):
        value = d_sum[s].total()

        def keep():
            g2[:, column(2 + s)] = value

        when(me != 3 if s == 0 else True, keep)

        @pl.when(d_apart(s))
        def _():
            d_turn[s] = value.T.astype(bf16)
            d_mirror_copy(s, me).start()

    def d_mirrored(s):
        @pl.when(me == 2 + s)
        def _():
            for slot in range(n):
                if slot != 3 and slot != 2 + s:
                    remote(
                        d_turn.at[s], d_turned.at[s, slot], d_mirror_send.at[s],
                        d_mirror_recv.at[s, slot], me_col, partner,
                    ).wait_recv()
                    g2[:, column(slot)] = d_turned[s, slot].astype(f32)

    d_finish(1)
    d_finish(0)
    for k in (1, 2, 3):
        a_mirror_copy(k).wait_recv()
        g1[:, column(lax.rem(me + n - k, n))] = a_turned[k - 1].astype(f32)

    @pl.when(z >= 2)
    def _():
        b_mirror_copy().wait_recv()
        g2[:, column(4 + lax.rem(me + 3, 4))] = b_turned[...].astype(f32)

    @pl.when(z == 0)
    def _():
        for slot in range(4):
            remote(
                c_turn.at[0], c_turned.at[slot], c_mirror_send.at[0], c_mirror_recv.at[slot],
                me_col, partner,
            ).wait_recv()
            g2[:, column(4 + slot)] = c_turned[slot].astype(f32)

    d_mirrored(0)
    d_mirrored(1)

    for k in range(3 * CHUNKS):
        left_copy(k).wait_send()
    for d in range(4):
        core_copy(a_part, a_peer, a_core, d).wait_send()
    for d in range(2):
        core_copy(b_part, b_peer, b_core, d).wait_send()
    for d in (0, 2, 3):
        core_copy(c_part, c_peer, c_core, d).wait_send()
    for s in range(2):
        for d in range(4):
            core_copy(d_part.at[s], d_peer.at[s], d_core.at[s], d).wait_send()
    for flow in (*a_sum, b_sum, c_sum, *d_sum):
        flow.drain()
    for k in (1, 2, 3):
        a_mirror_copy(k).wait_send()

    @pl.when(z >= 2)
    def _():
        b_mirror_copy().wait_send()
        for m in range(2):
            c_mirror_copy(m, me - 4).wait_send()

    for s in range(2):
        @pl.when(d_apart(s))
        def _():
            d_mirror_copy(s, me).wait_send()

    for step in range(1, n):
        e_copy(step).wait_send()


def general_kernel(
    n, n_col, x_hbm, rot_hbm, g1_hbm, g2_hbm, out_hbm,
    x, rot, left, pair, moved, part, peer, sums, landed,
    gram_out, energy, energy_in, shrunk,
    load_sem, left_send, left_recv, core_send, core_recv, z_send, z_recv,
    e_send, e_recv, store_sem, shrunk_sem,
):
    rows, width = x.shape
    half = width // 2
    block = width // n
    groups = n // 2
    total_rows = rows * n
    tiles = width // TILE
    row_tiles = rows // TILE
    per_tile = TILE // (2 * block)

    me_col = lax.axis_index("col")
    me = lax.axis_index("row")
    core = lax.rem(me, 2)
    group = lax.div(me, 2)
    partner = me + 1 - 2 * core

    def peer_at(step):
        return lax.rem(me + step, n)

    load_x = pltpu.make_async_copy(x_hbm, x, load_sem.at[0])
    load_r0 = [
        pltpu.make_async_copy(
            rot_hbm.at[0, :, pl.ds(h * half, half)], rot.at[0, :, pl.ds(h * half, half)],
            load_sem.at[1 + h],
        )
        for h in range(2)
    ]
    load_r1 = pltpu.make_async_copy(rot_hbm.at[1], rot.at[1], load_sem.at[3])
    load_x.start()
    load_r0[0].start()
    load_r0[1].start()
    load_r1.start()

    following = lax.rem(me_col + 1, n_col)
    preceding = lax.rem(me_col + n_col - 1, n_col)
    barrier = pltpu.get_barrier_semaphore()
    for other in (following, preceding):
        pl.semaphore_signal(
            barrier, inc=1, device_id={"col": other, "row": me},
            device_id_type=pl.DeviceIdType.MESH,
        )
    for step in range(1, n):
        pl.semaphore_signal(
            barrier, inc=1, device_id={"col": me_col, "row": peer_at(step)},
            device_id_type=pl.DeviceIdType.MESH,
        )

    def remote(src, dst, send_sem, recv_sem, col, row):
        return pltpu.make_async_remote_copy(
            src_ref=src, dst_ref=dst, send_sem=send_sem, recv_sem=recv_sem,
            device_id={"col": col, "row": row}, device_id_type=pl.DeviceIdType.MESH,
        )

    def turn(into, first, column):
        def body(t, _):
            span = pl.ds(pl.multiple_of(t * TILE, TILE), TILE)
            into[span, pl.ds(column - first, TILE)] = jnp.dot(
                x[span, :], rot[0, :, pl.ds(column, TILE)], preferred_element_type=jnp.float32
            ).astype(jnp.bfloat16)
            return 0
        lax.fori_loop(0, row_tiles, body, 0)

    pieces = half // TILE
    left_copy = [
        remote(
            left.at[:, pl.ds(h * TILE, TILE)], pair.at[:, pl.ds(h * TILE, TILE)],
            left_send.at[h], left_recv.at[h], following, me,
        )
        for h in range(pieces)
    ]
    load_x.wait()
    load_r0[0].wait()
    turn(left, 0, 0)
    pl.semaphore_wait(barrier, n + 1)
    left_copy[0].start()

    def z_copy(s, u):
        g = lax.rem(group + u, groups)
        k = lax.rem(g - group + 2 * groups - 1, groups)
        return remote(
            sums.at[s, g], landed.at[s, 0, k], z_send.at[s, k], z_recv.at[s, 0, k],
            me_col, 2 * g + core,
        )

    def added(s, u):
        return part[s, core, u].astype(jnp.float32) + peer[s, u].astype(jnp.float32)

    def rows_copy(s, q):
        span = pl.ds(q * per_tile, per_tile)
        return remote(
            part.at[s, 1 - core, span], peer.at[s, span],
            core_send.at[s, q], core_recv.at[s, q], me_col, partner,
        )

    def rows_terms(s, source):
        def body(q, _):
            turned_tile = source[:, pl.ds(pl.multiple_of(q * TILE, TILE), TILE)].T
            for m in range(tiles):
                term = jnp.dot(
                    turned_tile, source[:, m * TILE:(m + 1) * TILE],
                    preferred_element_type=jnp.float32,
                ).astype(jnp.bfloat16)
                for e in range(2 * per_tile):
                    part[s, e % 2, q * per_tile + e // 2, :, m * TILE:(m + 1) * TILE] = term[
                        e * block:(e + 1) * block, :
                    ]
            rows_copy(s, q).start()
            return 0
        lax.fori_loop(0, tiles, body, 0)

    def rows_pass(s):
        for q in range(tiles):
            rows_copy(s, q).wait_recv()

        def body(k, _):
            g = lax.rem(group + k, groups)
            sums[s, g] = added(s, g).astype(jnp.bfloat16)
            z_copy(s, k).start()
            return 0
        lax.fori_loop(1, groups, body, 0)

    def rows_sum(s):
        total = added(s, group)
        for k in range(1, groups):
            z_copy(s, k).wait_recv()
            total = total + landed[s, 0, k - 1].astype(jnp.float32)
        gram_out[s] = total / total_rows

    def gram_store(s, target):
        return pltpu.make_async_copy(gram_out.at[s], target, store_sem.at[s])

    rows_terms(0, x)
    for h in range(1, pieces):
        turn(left, 0, h * TILE)
        left_copy[h].start()
    rows_pass(0)
    load_r0[1].wait()
    for h in range(pieces):
        turn(pair, 0, half + h * TILE)
    load_r1.wait()

    def add_moved(first, depth, fresh):
        def body(t, acc):
            span = pl.ds(pl.multiple_of(t * TILE, TILE), TILE)
            value = jnp.dot(
                pair[span, pl.ds(first, depth)], rot[1, pl.ds(first, depth), :],
                preferred_element_type=jnp.float32,
            )
            if not fresh:
                value = value + moved[span, :]
            moved[span, :] = value
            return acc + jnp.sum(value * value, axis=0, keepdims=True)
        return lax.fori_loop(0, row_tiles, body, jnp.zeros((1, width), jnp.float32))

    add_moved(half, half, True)
    left_copy[0].wait_recv()
    for h in range(pieces - 1):
        if h > 0:
            left_copy[h].wait_recv()
        add_moved(h * TILE, TILE, False)
    rows_sum(0)
    gram_store(0, g1_hbm).start()
    left_copy[pieces - 1].wait_recv()
    rows_terms(1, pair)
    energy[...] = add_moved(half - TILE, TILE, False)

    def e_copy(step):
        return remote(
            energy, energy_in.at[step - 1], e_send.at[step - 1], e_recv.at[step - 1],
            me_col, peer_at(step),
        )

    for step in range(1, n):
        e_copy(step).start()
    rows_pass(1)
    total = energy[...]
    for step in range(1, n):
        e_copy(step).wait_recv()
        total = total + energy_in[step - 1]
    singular = jnp.sqrt(total / total_rows + 1e-06)
    factor = jnp.maximum(singular - 1.8, 0.0) / singular

    def out_copy(t):
        span = pl.ds(pl.multiple_of(t * TILE, TILE), TILE)
        return pltpu.make_async_copy(shrunk.at[span, :], out_hbm.at[span, :], shrunk_sem.at[t])

    def shrink(t, _):
        span = pl.ds(pl.multiple_of(t * TILE, TILE), TILE)
        shrunk[span, :] = (moved[span, :] * factor).astype(jnp.bfloat16)
        out_copy(t).start()
        return 0

    lax.fori_loop(0, row_tiles, shrink, 0)
    rows_sum(1)
    gram_store(1, g2_hbm).start()

    for h in range(pieces):
        left_copy[h].wait_send()
    for s in range(2):
        for q in range(tiles):
            rows_copy(s, q).wait_send()
        for k in range(1, groups):
            z_copy(s, k).wait_send()
    for step in range(1, n):
        e_copy(step).wait_send()
    for t in range(row_tiles):
        out_copy(t).wait()
    gram_store(0, g1_hbm).wait()
    gram_store(1, g2_hbm).wait()


def finish(*refs):
    sources, targets, sem = refs[:3], refs[3:6], refs[6]
    stores = [
        pltpu.make_async_copy(source, target, sem.at[at])
        for at, (source, target) in enumerate(zip(sources, targets))
    ]
    for store in stores:
        store.start()
    for store in stores:
        store.wait()


def general_scratch(n, rows, width):
    half = width // 2
    block = width // n
    groups = n // 2
    tiles = width // TILE
    sends = max(groups - 1, tiles)
    bf16, f32, dma = jnp.bfloat16, jnp.float32, pltpu.SemaphoreType.DMA
    return [
        pltpu.VMEM((rows, width), bf16),
        pltpu.VMEM((2, width, width), bf16),
        pltpu.VMEM((rows, half), bf16),
        pltpu.VMEM((rows, width), bf16),
        pltpu.VMEM((rows, width), f32),
        pltpu.VMEM((2, 2, groups, block, width), bf16),
        pltpu.VMEM((2, groups, block, width), bf16),
        pltpu.VMEM((2, groups, block, width), bf16),
        pltpu.VMEM((2, 1, groups - 1, block, width), bf16),
        pltpu.VMEM((2, block, width), f32),
        pltpu.VMEM((1, width), f32),
        pltpu.VMEM((n - 1, 1, width), f32),
        pltpu.VMEM((rows, width), bf16),
        dma((4,)),
        dma((half // TILE,)),
        dma((half // TILE,)),
        dma((2, sends)),
        dma((2, sends)),
        dma((2, sends)),
        dma((2, 1, groups - 1)),
        dma((n - 1,)),
        dma((n - 1,)),
        dma((2,)),
        dma((rows // TILE,)),
    ]


def paired_scratch(n, rows, width):
    half = width // 2
    bf16, f32, dma = jnp.bfloat16, jnp.float32, pltpu.SemaphoreType.DMA

    def room(*shape):
        return pltpu.VMEM(shape, bf16)

    return [
        room(rows, width),
        room(2, width, width),
        room(rows, half),
        room(rows, width),
        pltpu.VMEM((rows, width), f32),
        room(4, TILE, rows),
        room(width, rows),
        pltpu.VMEM((width, LANE), f32),
        room(2, 4, LANE, 5 * LANE),
        room(4, LANE, 5 * LANE),
        room(4, LANE, 5 * LANE),
        room(2, LANE, 5 * LANE),
        room(LANE, 5 * LANE),
        pltpu.VMEM((LANE, 5 * LANE), f32),
        room(3, LANE, LANE),
        room(3, LANE, LANE),
        room(2, 2, LANE, 3 * LANE),
        room(2, LANE, 3 * LANE),
        room(2, LANE, 3 * LANE),
        room(2, LANE, 3 * LANE),
        room(LANE, 3 * LANE),
        room(LANE, LANE),
        room(LANE, LANE),
        room(2, 4, LANE, TILE),
        room(4, LANE, TILE),
        room(4, LANE, TILE),
        room(2, LANE, TILE),
        room(LANE, TILE),
        room(2, LANE, LANE),
        room(4, LANE, LANE),
        room(2, 2, 4, LANE, LANE),
        room(2, 4, LANE, LANE),
        room(2, 4, LANE, LANE),
        room(2, LANE, LANE),
        room(LANE, LANE),
        room(3, LANE, LANE),
        room(2, LANE, LANE),
        room(2, n, LANE, LANE),
        pltpu.VMEM((1, width), f32),
        pltpu.VMEM((n - 1, 1, width), f32),
        dma((CHUNKS + 4,)),
        dma((3 * CHUNKS,)),
        dma((3 * CHUNKS,)),
        dma((2, 4)),
        dma((2, 4)),
        dma((2, 2)),
        dma((2, 3)),
        dma((2, 2)),
        dma((2, 2)),
        dma((2, 1)),
        dma((2,)),
        dma((2, 4)),
        dma((2, 2)),
        dma((2, 1)),
        dma((2,)),
        dma((4,)),
        dma((2, 2, 4)),
        dma((2, 2)),
        dma((2, 1)),
        dma((2, 3)),
        dma((2,)),
        dma((2, n)),
        dma((2, n - 1)),
    ]


def per_device(n, n_col, snapshots, rotations):
    rows, width = snapshots.shape
    block = width // n
    paired = n == 8 and block == LANE and rows % (CHUNKS * TILE) == 0
    bf16, f32 = jnp.bfloat16, jnp.float32
    anywhere = pl.BlockSpec(memory_space=pl.ANY)
    inside = pl.BlockSpec(memory_space=pltpu.VMEM)
    shapes = (
        jax.ShapeDtypeStruct((block, width), f32),
        jax.ShapeDtypeStruct((block, width), f32),
        jax.ShapeDtypeStruct((rows, width), bf16),
    )
    if paired:
        body = functools.partial(paired_kernel, n_col)
    else:
        body = functools.partial(general_kernel, n, n_col)
    results = pl.pallas_call(
        body,
        out_shape=tuple(pltpu.VMEM(shape.shape, shape.dtype) for shape in shapes),
        in_specs=[anywhere] * 2,
        out_specs=(inside if paired else anywhere,) * 3,
        scratch_shapes=(paired_scratch if paired else general_scratch)(n, rows, width),
        compiler_params=pltpu.CompilerParams(
            collective_id=0, has_side_effects=True, vmem_limit_bytes=44 * 1024 * 1024
        ),
    )(*(pltpu.with_memory_space_constraint(a, pltpu.HBM) for a in (snapshots, rotations)))
    return pl.pallas_call(
        finish,
        out_shape=shapes,
        in_specs=[anywhere] * 3,
        out_specs=(anywhere,) * 3,
        scratch_shapes=[pltpu.SemaphoreType.DMA((3,))],
    )(*(pltpu.with_memory_space_constraint(r, pltpu.VMEM) for r in results))


def solution(mesh):
    return jax.shard_map(
        functools.partial(per_device, mesh.shape["row"], mesh.shape["col"]),
        mesh=mesh,
        in_specs=(P("row", "col"), P(None, "col", None)),
        out_specs=(P(("col", "row"), None), P(("col", "row"), None), P("row", "col")),
        check_vma=False,
    )
```

```python
import functools

import jax
import jax.numpy as jnp
from jax import lax
from jax.experimental import pallas as pl
from jax.experimental.pallas import tpu as pltpu
from jax.sharding import PartitionSpec as P

TILE = 256
LANE = 128
CHUNKS = 4


def paired_kernel(
    n_col, x_hbm, rot_hbm, g1, g2, out,
    x, rot, left, pair, moved, flip_x, flip_l, flip_r, strip,
    a_part, a_peer, a_sums, a_near, a_far, a_total, a_turn, a_turned,
    l_part, l_peer, l_sums, l_near, l_far, l_turn, l_turned, l_row, l_in,
    b_part, b_peer, b_sums, b_near, b_far, b_turn, b_turned,
    c_part, c_peer, c_sums, c_near, c_far, c_turn, c_turned,
    d_part, d_peer, d_sums, d_near, d_far, d_turn, d_turned,
    h_part, h_peer, h_sums, h_land, h_out, h_row, h_col,
    energy, energy_in,
    load_sem, left_send, left_recv, a_core, a_first, a_second, a_mirror,
    l_core, l_first, l_second, l_mirror, l_sem,
    b_core, b_first, b_second, b_mirror,
    c_core, c_first, c_second, c_mirror_send, c_mirror_recv,
    d_core, d_first, d_second, d_mirror_send, d_mirror_recv,
    h_core, h_z, h_send, h_row_recv, h_col_recv, e_sem,
):
    n = 8
    rows, width = x.shape
    half = width // 2
    scale = 1.0 / (rows * n)
    chunk = rows // CHUNKS
    f32, bf16 = jnp.float32, jnp.bfloat16

    me_col = lax.axis_index("col")
    me = lax.axis_index("row")
    core = lax.rem(me, 2)
    z = lax.div(me, 2)
    partner = me + 1 - 2 * core
    beside = z + 1 - 2 * lax.rem(z, 2)
    across = 3 - z
    opposite = lax.rem(z + 2, 4)
    following = lax.rem(me_col + 1, n_col)
    preceding = lax.rem(me_col + n_col - 1, n_col)

    def rows_of(q):
        return pl.ds(q * chunk, chunk)

    def load(source, target, at):
        return pltpu.make_async_copy(source, target, load_sem.at[at])

    load_x = [load(x_hbm.at[rows_of(q)], x.at[rows_of(q)], q) for q in range(CHUNKS)]
    parts = ((0, 0, TILE), (0, TILE, TILE), (0, half, half), (1, 0, width))
    load_r = [
        load(
            rot_hbm.at[s, :, pl.ds(first, size)], rot.at[s, :, pl.ds(first, size)], CHUNKS + k
        )
        for k, (s, first, size) in enumerate(parts)
    ]
    load_x[0].start()
    load_r[0].start()
    for q in range(1, CHUNKS):
        load_x[q].start()
    for k in range(1, 4):
        load_r[k].start()

    barrier = pltpu.get_barrier_semaphore()
    for other in (following, preceding):
        pl.semaphore_signal(
            barrier, inc=1, device_id={"col": other, "row": me},
            device_id_type=pl.DeviceIdType.MESH,
        )
    for step in range(1, n):
        pl.semaphore_signal(
            barrier, inc=1, device_id={"col": me_col, "row": lax.rem(me + step, n)},
            device_id_type=pl.DeviceIdType.MESH,
        )

    def remote(src, dst, send_sem, recv_sem, col, row):
        return pltpu.make_async_remote_copy(
            src_ref=src, dst_ref=dst, send_sem=send_sem, recv_sem=recv_sem,
            device_id={"col": col, "row": row}, device_id_type=pl.DeviceIdType.MESH,
        )

    def to_chip(src, dst, sems, at, chip):
        return remote(src, dst, sems.at[0, at], sems.at[1, at], me_col, 2 * chip + core)

    def mul(a, b):
        return jnp.dot(a, b, preferred_element_type=f32)

    def when(condition, run):
        if condition is True:
            run()
        else:
            pl.when(condition)(run)

    def left_copy(k):
        q = k % CHUNKS
        first, size = ((0, TILE), (TILE, LANE), (TILE + LANE, LANE))[k // CHUNKS]
        here = (rows_of(q), pl.ds(first, size))
        return remote(
            left.at[here], pair.at[here], left_send.at[k], left_recv.at[k], following, me
        )

    load_r[0].wait()
    for q in range(CHUNKS):
        load_x[q].wait()
        left[rows_of(q), 0:TILE] = mul(x[rows_of(q), :], rot[0, :, 0:TILE]).astype(bf16)
        if q == 0:
            pl.semaphore_wait(barrier, n + 1)
        left_copy(q).start()

    def core_copy(part, peer, sems, at):
        return remote(
            part.at[1 - core, at], peer.at[at], sems.at[0, at], sems.at[1, at], me_col, partner
        )

    def added(part, peer, at, span):
        return part[core, at, span, :].astype(f32) + peer[at, span, :].astype(f32)

    class Fly:
        def __init__(self, part, peer, sums, near, far, near_sems, far_sems, base, span, first, second,
                     shift=0, live=lambda d: True):
            self.part, self.peer, self.sums, self.near, self.far = part, peer, sums, near, far
            self.near_sems, self.far_sems, self.base, self.span = near_sems, far_sems, base, span
            self.first, self.second, self.shift, self.live = first, second, shift, live

        def near_copy(self, slot, d):
            return to_chip(
                self.sums.at[d - self.shift, self.span], self.near.at[slot, self.span],
                self.near_sems, 2 * self.base + slot, self.first,
            )

        def far_copy(self):
            return to_chip(
                self.sums.at[self.second - self.shift, self.span], self.far.at[self.span],
                self.far_sems, self.base, self.second,
            )

        def term(self, d):
            return added(self.part, self.peer, d - self.shift, self.span)

        def send_near(self):
            for slot, d in enumerate((self.first, opposite)):
                def run(slot=slot, d=d):
                    self.sums[d - self.shift, self.span, :] = self.term(d).astype(bf16)
                    self.near_copy(slot, d).start()
                when(self.live(d), run)

        def send_far(self):
            def run():
                d = self.second
                self.near_copy(1, d).wait_recv()
                self.sums[d - self.shift, self.span, :] = (
                    self.term(d) + self.near[1, self.span, :].astype(f32)
                ).astype(bf16)
                self.far_copy().start()
            when(self.live(self.second), run)

        def total(self):
            self.near_copy(0, z).wait_recv()
            to_chip(
                self.sums.at[z - self.shift, self.span], self.far.at[self.span],
                self.far_sems, self.base, self.second,
            ).wait_recv()
            return (
                self.term(z) + self.near[0, self.span, :].astype(f32)
                + self.far[self.span, :].astype(f32)
            ) * scale

        def drain(self):
            for slot, d in enumerate((self.first, opposite)):
                when(self.live(d), lambda slot=slot, d=d: self.near_copy(slot, d).wait_send())
            when(self.live(self.second), lambda: self.far_copy().wait_send())

    everything = pl.ds(0, LANE)
    upper, lower = pl.ds(0, LANE // 2), pl.ds(LANE // 2, LANE // 2)
    a_sum = (
        Fly(a_part, a_peer, a_sums, a_near, a_far, a_first, a_second, 0, upper, beside, across),
        Fly(a_part, a_peer, a_sums, a_near, a_far, a_first, a_second, 1, lower, beside, across),
    )
    b_sum = Fly(
        b_part, b_peer, b_sums, b_near, b_far, b_first, b_second, 0, everything, beside, across,
        shift=2, live=lambda d: d >= 2,
    )

    class Direct:
        def __init__(self, part, peer, sums, land, sems):
            self.part, self.peer, self.sums, self.land, self.sems = part, peer, sums, land, sems

        def copy(self, slot, source, chip):
            return to_chip(self.sums.at[source], self.land.at[slot], self.sems, slot, chip)

        def send(self):
            for slot, d in enumerate((opposite, across, beside)):
                self.sums[d] = added(self.part, self.peer, d, slice(None)).astype(bf16)
                self.copy(slot, d, d).start()

        def total(self):
            value = added(self.part, self.peer, z, slice(None))
            for slot, d in ((2, beside), (1, across), (0, opposite)):
                self.copy(slot, z, d).wait_recv()
                value = value + self.land[slot].astype(f32)
            return value * scale

        def drain(self):
            for slot, d in enumerate((opposite, across, beside)):
                self.copy(slot, d, d).wait_send()

    l_sum = Fly(
        l_part, l_peer, l_sums, l_near, l_far, l_first, l_second, 0, everything, beside, across,
        live=lambda d: d < 2,
    )
    c_sum = Fly(
        c_part, c_peer, c_sums, c_near, c_far, c_first, c_second, 0, everything, beside, across,
        shift=2, live=lambda d: d >= 2,
    )
    d_sum = Fly(
        d_part, d_peer, d_sums, d_near, d_far, d_first, d_second, 0, everything, beside, across,
        shift=2, live=lambda d: d >= 2,
    )
    h_sum = Direct(h_part, h_peer, h_sums, h_land, h_z)

    def column(block):
        if isinstance(block, int):
            return pl.ds(block * LANE, LANE)
        return pl.ds(pl.multiple_of(block * LANE, LANE), LANE)

    for d in range(4):
        flip_x[d] = x[:, d * TILE:(d + 1) * TILE].T
        for k in range(3):
            m = (d + k) % 4
            term = mul(flip_x[d], x[:, m * TILE:(m + 1) * TILE]).astype(bf16)
            for e in range(2):
                for b in range(2):
                    slot = 2 * k + b - e
                    if 0 <= slot <= 4:
                        a_part[e, d, :, slot * LANE:(slot + 1) * LANE] = term[
                            e * LANE:(e + 1) * LANE, b * LANE:(b + 1) * LANE
                        ]
        core_copy(a_part, a_peer, a_core, d).start()

    load_r[1].wait()
    for q in range(CHUNKS):
        left[rows_of(q), TILE:half] = mul(x[rows_of(q), :], rot[0, :, TILE:half]).astype(bf16)
        left_copy(CHUNKS + q).start()
    for q in range(CHUNKS):
        left_copy(2 * CHUNKS + q).start()

    for d in range(4):
        core_copy(a_part, a_peer, a_core, d).wait_recv()
    for fly in a_sum:
        fly.send_near()
    def core_send(part, peer, sems, count):
        for d in range(count):
            core_copy(part, peer, sems, d).start()

    def core_wait(part, peer, sems, count):
        for d in range(count):
            core_copy(part, peer, sems, d).wait_recv()

    def ring_terms(source, first, flip, part, peer, sems):
        for d in range(2):
            flip[d * TILE:(d + 1) * TILE, :] = source[
                :, first + d * TILE:first + (d + 1) * TILE
            ].T
            term = mul(flip[d * TILE:(d + 1) * TILE, :], source[:, first:first + half]).astype(bf16)
            for e in range(2):
                for k in range(3):
                    at = (2 * d + e + k) % 4 * LANE
                    part[e, d, :, k * LANE:(k + 1) * LANE] = term[
                        e * LANE:(e + 1) * LANE, at:at + LANE
                    ]
            core_copy(part, peer, sems, d).start()

    ring_terms(left, 0, flip_l, l_part, l_peer, l_core)
    load_r[2].wait()

    def turn_right(first):
        def body(t, _):
            span = pl.ds(pl.multiple_of(t * TILE, TILE), TILE)
            pair[span, first:first + TILE] = mul(
                x[span, :], rot[0, :, first:first + TILE]
            ).astype(bf16)
            return 0
        lax.fori_loop(0, rows // TILE, body, 0)

    turn_right(half)
    core_wait(l_part, l_peer, l_core, 2)
    l_sum.send_near()
    turn_right(half + TILE)

    ring_terms(pair, half, flip_r, b_part, b_peer, b_core)
    load_r[3].wait()

    def move_right(t, _):
        span = pl.ds(pl.multiple_of(t * TILE, TILE), TILE)
        moved[span, :] = mul(pair[span, half:], rot[1, half:, :])
        return 0

    lax.fori_loop(0, rows // TILE // 2, move_right, 0)
    a_sum[0].send_far()
    core_wait(b_part, b_peer, b_core, 2)
    b_sum.send_near()
    lax.fori_loop(rows // TILE // 2, rows // TILE, move_right, 0)
    a_sum[1].send_far()

    def move_left(t, _):
        span = pl.ds(pl.multiple_of(t * TILE, TILE), TILE)
        moved[span, :] += mul(pair[span, 0:TILE], rot[1, 0:TILE, :])
        return 0

    for q in range(CHUNKS):
        left_copy(q).wait_recv()
    for d in range(2):
        term = mul(flip_r[d * TILE:(d + 1) * TILE, :], pair[:, 0:TILE]).astype(bf16)
        c_part[0, d] = term[:LANE]
        c_part[1, d] = term[LANE:]
        core_copy(c_part, c_peer, c_core, d).start()
    lax.fori_loop(0, rows // TILE, move_left, 0)
    core_wait(c_part, c_peer, c_core, 2)
    l_sum.send_far()
    b_sum.send_far()
    c_sum.send_near()

    for q in range(CHUNKS):
        left_copy(CHUNKS + q).wait_recv()
    term = mul(flip_r[...], pair[:, column(2)]).astype(bf16)
    for i in range(4):
        d_part[i % 2, i // 2] = term[i * LANE:(i + 1) * LANE]
    core_send(d_part, d_peer, d_core, 2)

    edge = half // n

    def strip_rows(q):
        span = rows_of(q)
        left_copy(2 * CHUNKS + q).wait_recv()
        value = mul(flip_r[:, q * chunk:(q + 1) * chunk], pair[span, column(3)])
        if q > 0:
            value = value + strip[...]
        if q < CHUNKS - 1:
            strip[...] = value
        else:
            for i in range(n):
                h_part[i % 2, i // 2] = value[i * edge:(i + 1) * edge].astype(bf16)
            core_send(h_part, h_peer, h_core, 4)

    def move_rows(q):
        span = rows_of(q)
        value = moved[span, :] + mul(pair[span, TILE:half], rot[1, TILE:half, :])
        moved[span, :] = value
        return jnp.sum(value * value, axis=0, keepdims=True)

    strip_rows(0)
    squares = move_rows(0)
    core_wait(d_part, d_peer, d_core, 2)
    d_sum.send_near()
    c_sum.send_far()

    def a_mirror_copy(k):
        return remote(
            a_turn.at[k - 1], a_turned.at[k - 1], a_mirror.at[0, k - 1], a_mirror.at[1, k - 1],
            me_col, lax.rem(me + k, n),
        )

    for fly in a_sum:
        a_total[fly.span, :] = fly.total()
    for k in (3, 2, 1):
        a_turn[k - 1] = a_total[:, k * LANE:(k + 1) * LANE].T.astype(bf16)
        a_mirror_copy(k).start()
    for k in range(5):
        g1[:, column(lax.rem(me + k, n))] = a_total[:, k * LANE:(k + 1) * LANE]

    for q in range(1, CHUNKS):
        strip_rows(q)
        squares = squares + move_rows(q)
    energy[...] = squares

    def e_copy(step):
        return remote(
            energy, energy_in.at[step - 1], e_sem.at[0, step - 1], e_sem.at[1, step - 1],
            me_col, lax.rem(me + step, n),
        )

    for step in range(1, n):
        e_copy(step).start()
    core_wait(h_part, h_peer, h_core, 4)
    h_sum.send()
    d_sum.send_far()

    def l_mirror_copy():
        return remote(
            l_turn, l_turned, l_mirror.at[0], l_mirror.at[1], me_col, lax.rem(me + 1, 4)
        )

    def l_copy(col):
        return remote(l_row, l_in, l_sem.at[0], l_sem.at[1], col, me)

    def b_mirror_copy():
        return remote(
            b_turn, b_turned, b_mirror.at[0], b_mirror.at[1], me_col, 4 + lax.rem(me + 1, 4)
        )

    def c_mirror_copy(m, slot):
        return remote(
            c_turn.at[m], c_turned.at[slot], c_mirror_send.at[m], c_mirror_recv.at[slot],
            me_col, m,
        )

    def d_mirror_copy(slot):
        return remote(
            d_turn, d_turned.at[slot], d_mirror_send.at[0], d_mirror_recv.at[slot], me_col, 2
        )

    @pl.when(z < 2)
    def _():
        value = l_sum.total()
        l_turn[...] = value[:, LANE:2 * LANE].T.astype(bf16)
        l_mirror_copy().start()
        for k in range(3):
            l_row[:, column(lax.rem(me + k, 4))] = value[:, k * LANE:(k + 1) * LANE].astype(bf16)

    @pl.when(z >= 2)
    def _():
        value = b_sum.total()
        b_turn[...] = value[:, LANE:2 * LANE].T.astype(bf16)
        b_mirror_copy().start()
        for k in range(3):
            g2[:, column(4 + lax.rem(me + k, 4))] = value[:, k * LANE:(k + 1) * LANE]
        value = c_sum.total()
        g2[:, 0:TILE] = value
        for m in range(2):
            c_turn[m] = value[:, m * LANE:(m + 1) * LANE].T.astype(bf16)
            c_mirror_copy(m, me - 4).start()

    @pl.when(z < 2)
    def _():
        l_mirror_copy().wait_recv()
        l_row[:, column(lax.rem(me + 3, 4))] = l_turned[...]
        l_copy(following).start()

    total = energy[...]
    for step in range(1, n):
        e_copy(step).wait_recv()
        total = total + energy_in[step - 1]
    singular = jnp.sqrt(total * scale + 1e-06)
    factor = jnp.maximum(singular - 1.8, 0.0) / singular

    def shrink(t, _):
        span = pl.ds(pl.multiple_of(t * TILE, TILE), TILE)
        out[span, :] = (moved[span, :] * factor).astype(bf16)
        return 0

    lax.fori_loop(0, rows // TILE, shrink, 0)

    def h_row_copy(slot, row):
        return remote(h_out, h_row.at[slot], h_send.at[0], h_row_recv.at[slot], me_col, row)

    def h_col_copy(slot, row):
        place = slot * edge if isinstance(slot, int) else pl.multiple_of(slot * edge, edge)
        return remote(
            h_out, h_col.at[pl.ds(place, edge)], h_send.at[1], h_col_recv.at[slot], me_col, row
        )

    value = h_sum.total()
    h_out[...] = value.astype(bf16)

    @pl.when(me != 3)
    def _():
        h_col_copy(me, 3).start()

    @pl.when(me != 7)
    def _():
        h_row_copy(core, 4 + z).start()

    @pl.when(me == 3)
    def _():
        h_col[3 * edge:4 * edge, :] = value.astype(bf16)

    @pl.when(z >= 2)
    def _():
        value = d_sum.total()
        g2[:, column(2)] = value
        d_turn[...] = value.T.astype(bf16)
        d_mirror_copy(me - 4).start()

    for k in (1, 2, 3):
        a_mirror_copy(k).wait_recv()
        g1[:, column(lax.rem(me + n - k, n))] = a_turned[k - 1].astype(f32)

    @pl.when(z >= 2)
    def _():
        b_mirror_copy().wait_recv()
        g2[:, column(4 + lax.rem(me + 3, 4))] = b_turned[...].astype(f32)

    @pl.when(z < 2)
    def _():
        l_copy(preceding).wait_recv()
        g2[:, 0:half] = l_in[...].astype(f32)

    @pl.when(z == 0)
    def _():
        for slot in range(4):
            remote(
                c_turn.at[0], c_turned.at[slot], c_mirror_send.at[0], c_mirror_recv.at[slot],
                me_col, partner,
            ).wait_recv()
            g2[:, column(4 + slot)] = c_turned[slot].astype(f32)

    @pl.when(me == 2)
    def _():
        for slot in range(4):
            remote(
                d_turn, d_turned.at[slot], d_mirror_send.at[0], d_mirror_recv.at[slot],
                me_col, partner,
            ).wait_recv()
            g2[:, column(4 + slot)] = d_turned[slot].astype(f32)

    @pl.when(z >= 2)
    def _():
        h_row_copy(0, partner).wait_recv()
        g2[0:edge, column(3)] = h_row[0].astype(f32)

    @pl.when((z >= 2) & (me != 7))
    def _():
        h_row_copy(1, partner).wait_recv()
        g2[edge:2 * edge, column(3)] = h_row[1].astype(f32)

    @pl.when(me == 7)
    def _():
        g2[edge:2 * edge, column(3)] = value

    @pl.when(me == 3)
    def _():
        for slot in range(n):
            if slot != 3:
                h_col_copy(slot, partner).wait_recv()
        for block in range(4):
            g2[:, column(4 + block)] = h_col[block * LANE:(block + 1) * LANE, :].T.astype(f32)

    for k in range(3 * CHUNKS):
        left_copy(k).wait_send()
    for part, peer, sems, count in (
        (a_part, a_peer, a_core, 4), (l_part, l_peer, l_core, 2), (b_part, b_peer, b_core, 2),
        (c_part, c_peer, c_core, 2), (d_part, d_peer, d_core, 2), (h_part, h_peer, h_core, 4),
    ):
        for d in range(count):
            core_copy(part, peer, sems, d).wait_send()
    for flow in (*a_sum, l_sum, b_sum, c_sum, d_sum, h_sum):
        flow.drain()
    for k in (1, 2, 3):
        a_mirror_copy(k).wait_send()

    @pl.when(z < 2)
    def _():
        l_mirror_copy().wait_send()
        l_copy(following).wait_send()

    @pl.when(z >= 2)
    def _():
        b_mirror_copy().wait_send()
        for m in range(2):
            c_mirror_copy(m, me - 4).wait_send()
        d_mirror_copy(me - 4).wait_send()

    @pl.when(me != 3)
    def _():
        h_col_copy(me, 3).wait_send()

    @pl.when(me != 7)
    def _():
        h_row_copy(core, 4 + z).wait_send()

    for step in range(1, n):
        e_copy(step).wait_send()


def general_kernel(
    n, n_col, x_hbm, rot_hbm, g1_hbm, g2_hbm, out_hbm,
    x, rot, left, pair, moved, part, peer, sums, landed,
    gram_out, energy, energy_in, shrunk,
    load_sem, left_send, left_recv, core_send, core_recv, z_send, z_recv,
    e_send, e_recv, store_sem, shrunk_sem,
):
    rows, width = x.shape
    half = width // 2
    block = width // n
    groups = n // 2
    total_rows = rows * n
    tiles = width // TILE
    row_tiles = rows // TILE
    per_tile = TILE // (2 * block)

    me_col = lax.axis_index("col")
    me = lax.axis_index("row")
    core = lax.rem(me, 2)
    group = lax.div(me, 2)
    partner = me + 1 - 2 * core

    def peer_at(step):
        return lax.rem(me + step, n)

    load_x = pltpu.make_async_copy(x_hbm, x, load_sem.at[0])
    load_r0 = [
        pltpu.make_async_copy(
            rot_hbm.at[0, :, pl.ds(h * half, half)], rot.at[0, :, pl.ds(h * half, half)],
            load_sem.at[1 + h],
        )
        for h in range(2)
    ]
    load_r1 = pltpu.make_async_copy(rot_hbm.at[1], rot.at[1], load_sem.at[3])
    load_x.start()
    load_r0[0].start()
    load_r0[1].start()
    load_r1.start()

    following = lax.rem(me_col + 1, n_col)
    preceding = lax.rem(me_col + n_col - 1, n_col)
    barrier = pltpu.get_barrier_semaphore()
    for other in (following, preceding):
        pl.semaphore_signal(
            barrier, inc=1, device_id={"col": other, "row": me},
            device_id_type=pl.DeviceIdType.MESH,
        )
    for step in range(1, n):
        pl.semaphore_signal(
            barrier, inc=1, device_id={"col": me_col, "row": peer_at(step)},
            device_id_type=pl.DeviceIdType.MESH,
        )

    def remote(src, dst, send_sem, recv_sem, col, row):
        return pltpu.make_async_remote_copy(
            src_ref=src, dst_ref=dst, send_sem=send_sem, recv_sem=recv_sem,
            device_id={"col": col, "row": row}, device_id_type=pl.DeviceIdType.MESH,
        )

    def turn(into, first, column):
        def body(t, _):
            span = pl.ds(pl.multiple_of(t * TILE, TILE), TILE)
            into[span, pl.ds(column - first, TILE)] = jnp.dot(
                x[span, :], rot[0, :, pl.ds(column, TILE)], preferred_element_type=jnp.float32
            ).astype(jnp.bfloat16)
            return 0
        lax.fori_loop(0, row_tiles, body, 0)

    pieces = half // TILE
    left_copy = [
        remote(
            left.at[:, pl.ds(h * TILE, TILE)], pair.at[:, pl.ds(h * TILE, TILE)],
            left_send.at[h], left_recv.at[h], following, me,
        )
        for h in range(pieces)
    ]
    load_x.wait()
    load_r0[0].wait()
    turn(left, 0, 0)
    pl.semaphore_wait(barrier, n + 1)
    left_copy[0].start()

    def z_copy(s, u):
        g = lax.rem(group + u, groups)
        k = lax.rem(g - group + 2 * groups - 1, groups)
        return remote(
            sums.at[s, g], landed.at[s, 0, k], z_send.at[s, k], z_recv.at[s, 0, k],
            me_col, 2 * g + core,
        )

    def added(s, u):
        return part[s, core, u].astype(jnp.float32) + peer[s, u].astype(jnp.float32)

    def rows_copy(s, q):
        span = pl.ds(q * per_tile, per_tile)
        return remote(
            part.at[s, 1 - core, span], peer.at[s, span],
            core_send.at[s, q], core_recv.at[s, q], me_col, partner,
        )

    def rows_terms(s, source):
        def body(q, _):
            turned_tile = source[:, pl.ds(pl.multiple_of(q * TILE, TILE), TILE)].T
            for m in range(tiles):
                term = jnp.dot(
                    turned_tile, source[:, m * TILE:(m + 1) * TILE],
                    preferred_element_type=jnp.float32,
                ).astype(jnp.bfloat16)
                for e in range(2 * per_tile):
                    part[s, e % 2, q * per_tile + e // 2, :, m * TILE:(m + 1) * TILE] = term[
                        e * block:(e + 1) * block, :
                    ]
            rows_copy(s, q).start()
            return 0
        lax.fori_loop(0, tiles, body, 0)

    def rows_pass(s):
        for q in range(tiles):
            rows_copy(s, q).wait_recv()

        def body(k, _):
            g = lax.rem(group + k, groups)
            sums[s, g] = added(s, g).astype(jnp.bfloat16)
            z_copy(s, k).start()
            return 0
        lax.fori_loop(1, groups, body, 0)

    def rows_sum(s):
        total = added(s, group)
        for k in range(1, groups):
            z_copy(s, k).wait_recv()
            total = total + landed[s, 0, k - 1].astype(jnp.float32)
        gram_out[s] = total / total_rows

    def gram_store(s, target):
        return pltpu.make_async_copy(gram_out.at[s], target, store_sem.at[s])

    rows_terms(0, x)
    for h in range(1, pieces):
        turn(left, 0, h * TILE)
        left_copy[h].start()
    rows_pass(0)
    load_r0[1].wait()
    for h in range(pieces):
        turn(pair, 0, half + h * TILE)
    load_r1.wait()

    def add_moved(first, depth, fresh):
        def body(t, acc):
            span = pl.ds(pl.multiple_of(t * TILE, TILE), TILE)
            value = jnp.dot(
                pair[span, pl.ds(first, depth)], rot[1, pl.ds(first, depth), :],
                preferred_element_type=jnp.float32,
            )
            if not fresh:
                value = value + moved[span, :]
            moved[span, :] = value
            return acc + jnp.sum(value * value, axis=0, keepdims=True)
        return lax.fori_loop(0, row_tiles, body, jnp.zeros((1, width), jnp.float32))

    add_moved(half, half, True)
    left_copy[0].wait_recv()
    for h in range(pieces - 1):
        if h > 0:
            left_copy[h].wait_recv()
        add_moved(h * TILE, TILE, False)
    rows_sum(0)
    gram_store(0, g1_hbm).start()
    left_copy[pieces - 1].wait_recv()
    rows_terms(1, pair)
    energy[...] = add_moved(half - TILE, TILE, False)

    def e_copy(step):
        return remote(
            energy, energy_in.at[step - 1], e_send.at[step - 1], e_recv.at[step - 1],
            me_col, peer_at(step),
        )

    for step in range(1, n):
        e_copy(step).start()
    rows_pass(1)
    total = energy[...]
    for step in range(1, n):
        e_copy(step).wait_recv()
        total = total + energy_in[step - 1]
    singular = jnp.sqrt(total / total_rows + 1e-06)
    factor = jnp.maximum(singular - 1.8, 0.0) / singular

    def out_copy(t):
        span = pl.ds(pl.multiple_of(t * TILE, TILE), TILE)
        return pltpu.make_async_copy(shrunk.at[span, :], out_hbm.at[span, :], shrunk_sem.at[t])

    def shrink(t, _):
        span = pl.ds(pl.multiple_of(t * TILE, TILE), TILE)
        shrunk[span, :] = (moved[span, :] * factor).astype(jnp.bfloat16)
        out_copy(t).start()
        return 0

    lax.fori_loop(0, row_tiles, shrink, 0)
    rows_sum(1)
    gram_store(1, g2_hbm).start()

    for h in range(pieces):
        left_copy[h].wait_send()
    for s in range(2):
        for q in range(tiles):
            rows_copy(s, q).wait_send()
        for k in range(1, groups):
            z_copy(s, k).wait_send()
    for step in range(1, n):
        e_copy(step).wait_send()
    for t in range(row_tiles):
        out_copy(t).wait()
    gram_store(0, g1_hbm).wait()
    gram_store(1, g2_hbm).wait()


def finish(*refs):
    sources, targets, sem = refs[:3], refs[3:6], refs[6]
    stores = [
        pltpu.make_async_copy(source, target, sem.at[at])
        for at, (source, target) in enumerate(zip(sources, targets))
    ]
    for store in stores:
        store.start()
    for store in stores:
        store.wait()


def general_scratch(n, rows, width):
    half = width // 2
    block = width // n
    groups = n // 2
    tiles = width // TILE
    sends = max(groups - 1, tiles)
    bf16, f32, dma = jnp.bfloat16, jnp.float32, pltpu.SemaphoreType.DMA
    return [
        pltpu.VMEM((rows, width), bf16),
        pltpu.VMEM((2, width, width), bf16),
        pltpu.VMEM((rows, half), bf16),
        pltpu.VMEM((rows, width), bf16),
        pltpu.VMEM((rows, width), f32),
        pltpu.VMEM((2, 2, groups, block, width), bf16),
        pltpu.VMEM((2, groups, block, width), bf16),
        pltpu.VMEM((2, groups, block, width), bf16),
        pltpu.VMEM((2, 1, groups - 1, block, width), bf16),
        pltpu.VMEM((2, block, width), f32),
        pltpu.VMEM((1, width), f32),
        pltpu.VMEM((n - 1, 1, width), f32),
        pltpu.VMEM((rows, width), bf16),
        dma((4,)),
        dma((half // TILE,)),
        dma((half // TILE,)),
        dma((2, sends)),
        dma((2, sends)),
        dma((2, sends)),
        dma((2, 1, groups - 1)),
        dma((n - 1,)),
        dma((n - 1,)),
        dma((2,)),
        dma((rows // TILE,)),
    ]


def paired_scratch(n, rows, width):
    half = width // 2
    bf16, f32, dma = jnp.bfloat16, jnp.float32, pltpu.SemaphoreType.DMA

    def room(*shape):
        return pltpu.VMEM(shape, bf16)

    return [
        room(rows, width),
        room(2, width, width),
        room(rows, half),
        room(rows, width),
        pltpu.VMEM((rows, width), f32),
        room(4, TILE, rows),
        room(half, rows),
        room(half, rows),
        pltpu.VMEM((half, LANE), f32),
        room(2, 4, LANE, 5 * LANE),
        room(4, LANE, 5 * LANE),
        room(4, LANE, 5 * LANE),
        room(2, LANE, 5 * LANE),
        room(LANE, 5 * LANE),
        pltpu.VMEM((LANE, 5 * LANE), f32),
        room(3, LANE, LANE),
        room(3, LANE, LANE),
        room(2, 2, LANE, 3 * LANE),
        room(2, LANE, 3 * LANE),
        room(2, LANE, 3 * LANE),
        room(2, LANE, 3 * LANE),
        room(LANE, 3 * LANE),
        room(LANE, LANE),
        room(LANE, LANE),
        room(LANE, half),
        room(LANE, half),
        room(2, 2, LANE, 3 * LANE),
        room(2, LANE, 3 * LANE),
        room(2, LANE, 3 * LANE),
        room(2, LANE, 3 * LANE),
        room(LANE, 3 * LANE),
        room(LANE, LANE),
        room(LANE, LANE),
        room(2, 2, LANE, TILE),
        room(2, LANE, TILE),
        room(2, LANE, TILE),
        room(2, LANE, TILE),
        room(LANE, TILE),
        room(2, LANE, LANE),
        room(4, LANE, LANE),
        room(2, 2, LANE, LANE),
        room(2, LANE, LANE),
        room(2, LANE, LANE),
        room(2, LANE, LANE),
        room(LANE, LANE),
        room(LANE, LANE),
        room(4, LANE, LANE),
        room(2, 4, half // n, LANE),
        room(4, half // n, LANE),
        room(4, half // n, LANE),
        room(3, half // n, LANE),
        room(half // n, LANE),
        room(2, half // n, LANE),
        room(half, LANE),
        pltpu.VMEM((1, width), f32),
        pltpu.VMEM((n - 1, 1, width), f32),
        dma((CHUNKS + 4,)),
        dma((3 * CHUNKS,)),
        dma((3 * CHUNKS,)),
        dma((2, 4)),
        dma((2, 4)),
        dma((2, 2)),
        dma((2, 3)),
        dma((2, 2)),
        dma((2, 2)),
        dma((2, 1)),
        dma((2,)),
        dma((2,)),
        dma((2, 2)),
        dma((2, 2)),
        dma((2, 1)),
        dma((2,)),
        dma((2, 2)),
        dma((2, 2)),
        dma((2, 1)),
        dma((2,)),
        dma((4,)),
        dma((2, 2)),
        dma((2, 2)),
        dma((2, 1)),
        dma((1,)),
        dma((4,)),
        dma((2, 4)),
        dma((2, 3)),
        dma((2,)),
        dma((2,)),
        dma((n,)),
        dma((2, n - 1)),
    ]


def per_device(n, n_col, snapshots, rotations):
    rows, width = snapshots.shape
    block = width // n
    paired = n == 8 and block == LANE and rows % (CHUNKS * TILE) == 0
    bf16, f32 = jnp.bfloat16, jnp.float32
    anywhere = pl.BlockSpec(memory_space=pl.ANY)
    inside = pl.BlockSpec(memory_space=pltpu.VMEM)
    shapes = (
        jax.ShapeDtypeStruct((block, width), f32),
        jax.ShapeDtypeStruct((block, width), f32),
        jax.ShapeDtypeStruct((rows, width), bf16),
    )
    if paired:
        body = functools.partial(paired_kernel, n_col)
    else:
        body = functools.partial(general_kernel, n, n_col)
    results = pl.pallas_call(
        body,
        out_shape=tuple(pltpu.VMEM(shape.shape, shape.dtype) for shape in shapes),
        in_specs=[anywhere] * 2,
        out_specs=(inside if paired else anywhere,) * 3,
        scratch_shapes=(paired_scratch if paired else general_scratch)(n, rows, width),
        compiler_params=pltpu.CompilerParams(
            collective_id=0, has_side_effects=True, vmem_limit_bytes=44 * 1024 * 1024
        ),
    )(*(pltpu.with_memory_space_constraint(a, pltpu.HBM) for a in (snapshots, rotations)))
    return pl.pallas_call(
        finish,
        out_shape=shapes,
        in_specs=[anywhere] * 3,
        out_specs=(anywhere,) * 3,
        scratch_shapes=[pltpu.SemaphoreType.DMA((3,))],
    )(*(pltpu.with_memory_space_constraint(r, pltpu.VMEM) for r in results))


def solution(mesh):
    return jax.shard_map(
        functools.partial(per_device, mesh.shape["row"], mesh.shape["col"]),
        mesh=mesh,
        in_specs=(P("row", "col"), P(None, "col", None)),
        out_specs=(P(("col", "row"), None), P(("col", "row"), None), P("row", "col")),
        check_vma=False,
    )
```

```python
import functools

import jax
import jax.numpy as jnp
from jax import lax
from jax.experimental import pallas as pl
from jax.experimental.pallas import tpu as pltpu
from jax.sharding import PartitionSpec as P

TILE = 256
LANE = 128
CHUNKS = 4


def paired_kernel(
    n_col, x_hbm, rot_hbm, g1, g2, out,
    x, rot, left, pair, moved, flip_x, flip_l, flip_r, strip,
    a_part, a_peer, a_sums, a_near, a_far, a_total, a_turn, a_turned,
    l_part, l_peer, l_sums, l_near, l_far, l_turn, l_turned, l_row, l_in,
    b_part, b_peer, b_sums, b_near, b_far, b_turn, b_turned,
    c_part, c_peer, c_sums, c_near, c_far, c_turn, c_turned,
    d_part, d_peer, d_sums, d_near, d_far, d_turn, d_turned,
    h_part, h_peer, h_sums, h_land, h_out, h_row, h_col,
    energy, energy_in,
    load_sem, left_send, left_recv, a_core, a_first, a_second, a_mirror,
    l_core, l_first, l_second, l_mirror, l_sem,
    b_core, b_first, b_second, b_mirror,
    c_core, c_first, c_second, c_mirror_send, c_mirror_recv,
    d_core, d_first, d_second, d_mirror_send, d_mirror_recv,
    h_core, h_z, h_send, h_row_recv, h_col_recv, e_sem,
):
    n = 8
    rows, width = x.shape
    half = width // 2
    scale = 1.0 / (rows * n)
    chunk = rows // CHUNKS
    f32, bf16 = jnp.float32, jnp.bfloat16

    me_col = lax.axis_index("col")
    me = lax.axis_index("row")
    core = lax.rem(me, 2)
    z = lax.div(me, 2)
    partner = me + 1 - 2 * core
    beside = z + 1 - 2 * lax.rem(z, 2)
    across = 3 - z
    opposite = lax.rem(z + 2, 4)
    following = lax.rem(me_col + 1, n_col)
    preceding = lax.rem(me_col + n_col - 1, n_col)

    def rows_of(q):
        return pl.ds(q * chunk, chunk)

    def load(source, target, at):
        return pltpu.make_async_copy(source, target, load_sem.at[at])

    load_x = [load(x_hbm.at[rows_of(q)], x.at[rows_of(q)], q) for q in range(CHUNKS)]
    parts = ((0, 0, TILE), (0, TILE, TILE), (0, half, half), (1, 0, width))
    load_r = [
        load(
            rot_hbm.at[s, :, pl.ds(first, size)], rot.at[s, :, pl.ds(first, size)], CHUNKS + k
        )
        for k, (s, first, size) in enumerate(parts)
    ]
    load_x[0].start()
    load_r[0].start()
    for q in range(1, CHUNKS):
        load_x[q].start()
    for k in range(1, 4):
        load_r[k].start()

    barrier = pltpu.get_barrier_semaphore()
    for other in (following, preceding):
        pl.semaphore_signal(
            barrier, inc=1, device_id={"col": other, "row": me},
            device_id_type=pl.DeviceIdType.MESH,
        )
    for step in range(1, n):
        pl.semaphore_signal(
            barrier, inc=1, device_id={"col": me_col, "row": lax.rem(me + step, n)},
            device_id_type=pl.DeviceIdType.MESH,
        )

    def remote(src, dst, send_sem, recv_sem, col, row):
        return pltpu.make_async_remote_copy(
            src_ref=src, dst_ref=dst, send_sem=send_sem, recv_sem=recv_sem,
            device_id={"col": col, "row": row}, device_id_type=pl.DeviceIdType.MESH,
        )

    def to_chip(src, dst, sems, at, chip):
        return remote(src, dst, sems.at[0, at], sems.at[1, at], me_col, 2 * chip + core)

    def mul(a, b):
        return jnp.dot(a, b, preferred_element_type=f32)

    def when(condition, run):
        if condition is True:
            run()
        else:
            pl.when(condition)(run)

    def left_copy(k):
        q = k % CHUNKS
        first, size = ((0, TILE), (TILE, LANE), (TILE + LANE, LANE))[k // CHUNKS]
        here = (rows_of(q), pl.ds(first, size))
        return remote(
            left.at[here], pair.at[here], left_send.at[k], left_recv.at[k], following, me
        )

    load_r[0].wait()
    for q in range(CHUNKS):
        load_x[q].wait()
        left[rows_of(q), 0:TILE] = mul(x[rows_of(q), :], rot[0, :, 0:TILE]).astype(bf16)
        if q == 0:
            pl.semaphore_wait(barrier, n + 1)
        left_copy(q).start()

    def core_copy(part, peer, sems, at):
        return remote(
            part.at[1 - core, at], peer.at[at], sems.at[0, at], sems.at[1, at], me_col, partner
        )

    def added(part, peer, at, span):
        return part[core, at, span, :].astype(f32) + peer[at, span, :].astype(f32)

    class Fly:
        def __init__(self, part, peer, sums, near, far, near_sems, far_sems, base, span, first, second,
                     shift=0, live=lambda d: True):
            self.part, self.peer, self.sums, self.near, self.far = part, peer, sums, near, far
            self.near_sems, self.far_sems, self.base, self.span = near_sems, far_sems, base, span
            self.first, self.second, self.shift, self.live = first, second, shift, live

        def near_copy(self, slot, d):
            return to_chip(
                self.sums.at[d - self.shift, self.span], self.near.at[slot, self.span],
                self.near_sems, 2 * self.base + slot, self.first,
            )

        def far_copy(self):
            return to_chip(
                self.sums.at[self.second - self.shift, self.span], self.far.at[self.span],
                self.far_sems, self.base, self.second,
            )

        def term(self, d):
            return added(self.part, self.peer, d - self.shift, self.span)

        def send_near(self):
            for slot, d in enumerate((self.first, opposite)):
                def run(slot=slot, d=d):
                    self.sums[d - self.shift, self.span, :] = self.term(d).astype(bf16)
                    self.near_copy(slot, d).start()
                when(self.live(d), run)

        def send_far(self):
            def run():
                d = self.second
                self.near_copy(1, d).wait_recv()
                self.sums[d - self.shift, self.span, :] = (
                    self.term(d) + self.near[1, self.span, :].astype(f32)
                ).astype(bf16)
                self.far_copy().start()
            when(self.live(self.second), run)

        def total(self):
            self.near_copy(0, z).wait_recv()
            to_chip(
                self.sums.at[z - self.shift, self.span], self.far.at[self.span],
                self.far_sems, self.base, self.second,
            ).wait_recv()
            return (
                self.term(z) + self.near[0, self.span, :].astype(f32)
                + self.far[self.span, :].astype(f32)
            ) * scale

        def drain(self):
            for slot, d in enumerate((self.first, opposite)):
                when(self.live(d), lambda slot=slot, d=d: self.near_copy(slot, d).wait_send())
            when(self.live(self.second), lambda: self.far_copy().wait_send())

    everything = pl.ds(0, LANE)
    upper, lower = pl.ds(0, LANE // 2), pl.ds(LANE // 2, LANE // 2)
    a_sum = (
        Fly(a_part, a_peer, a_sums, a_near, a_far, a_first, a_second, 0, upper, beside, across),
        Fly(a_part, a_peer, a_sums, a_near, a_far, a_first, a_second, 1, lower, beside, across),
    )
    b_sum = Fly(
        b_part, b_peer, b_sums, b_near, b_far, b_first, b_second, 0, everything, beside, across,
        shift=2, live=lambda d: d >= 2,
    )

    class Direct:
        def __init__(self, part, peer, sums, land, sems):
            self.part, self.peer, self.sums, self.land, self.sems = part, peer, sums, land, sems

        def copy(self, slot, source, chip):
            return to_chip(self.sums.at[source], self.land.at[slot], self.sems, slot, chip)

        def send(self):
            for slot, d in enumerate((opposite, across, beside)):
                self.sums[d] = added(self.part, self.peer, d, slice(None)).astype(bf16)
                self.copy(slot, d, d).start()

        def total(self):
            value = added(self.part, self.peer, z, slice(None))
            for slot, d in ((2, beside), (1, across), (0, opposite)):
                self.copy(slot, z, d).wait_recv()
                value = value + self.land[slot].astype(f32)
            return value * scale

        def drain(self):
            for slot, d in enumerate((opposite, across, beside)):
                self.copy(slot, d, d).wait_send()

    l_sum = Fly(
        l_part, l_peer, l_sums, l_near, l_far, l_first, l_second, 0, everything, beside, across,
        live=lambda d: d < 2,
    )
    c_sum = Fly(
        c_part, c_peer, c_sums, c_near, c_far, c_first, c_second, 0, everything, beside, across,
        shift=2, live=lambda d: d >= 2,
    )
    d_sum = Fly(
        d_part, d_peer, d_sums, d_near, d_far, d_first, d_second, 0, everything, beside, across,
        shift=2, live=lambda d: d >= 2,
    )
    h_sum = Direct(h_part, h_peer, h_sums, h_land, h_z)

    def column(block):
        if isinstance(block, int):
            return pl.ds(block * LANE, LANE)
        return pl.ds(pl.multiple_of(block * LANE, LANE), LANE)

    for d in range(4):
        flip_x[d] = x[:, d * TILE:(d + 1) * TILE].T
        for k in range(3):
            m = (d + k) % 4
            term = mul(flip_x[d], x[:, m * TILE:(m + 1) * TILE]).astype(bf16)
            for e in range(2):
                for b in range(2):
                    slot = 2 * k + b - e
                    if 0 <= slot <= 4:
                        a_part[e, d, :, slot * LANE:(slot + 1) * LANE] = term[
                            e * LANE:(e + 1) * LANE, b * LANE:(b + 1) * LANE
                        ]
        core_copy(a_part, a_peer, a_core, d).start()

    load_r[1].wait()
    for q in range(CHUNKS):
        left[rows_of(q), TILE:half] = mul(x[rows_of(q), :], rot[0, :, TILE:half]).astype(bf16)
        left_copy(CHUNKS + q).start()
    for q in range(CHUNKS):
        left_copy(2 * CHUNKS + q).start()

    for d in range(4):
        core_copy(a_part, a_peer, a_core, d).wait_recv()
    a_sum[0].send_near()
    def core_send(part, peer, sems, count):
        for d in range(count):
            core_copy(part, peer, sems, d).start()

    def core_wait(part, peer, sems, count):
        for d in range(count):
            core_copy(part, peer, sems, d).wait_recv()

    def ring_terms(source, first, flip, part, peer, sems):
        for d in range(2):
            flip[d * TILE:(d + 1) * TILE, :] = source[
                :, first + d * TILE:first + (d + 1) * TILE
            ].T
            term = mul(flip[d * TILE:(d + 1) * TILE, :], source[:, first:first + half]).astype(bf16)
            for e in range(2):
                for k in range(3):
                    at = (2 * d + e + k) % 4 * LANE
                    part[e, d, :, k * LANE:(k + 1) * LANE] = term[
                        e * LANE:(e + 1) * LANE, at:at + LANE
                    ]
            core_copy(part, peer, sems, d).start()

    ring_terms(left, 0, flip_l, l_part, l_peer, l_core)
    load_r[2].wait()

    def turn_right(first):
        def body(t, _):
            span = pl.ds(pl.multiple_of(t * TILE, TILE), TILE)
            pair[span, first:first + TILE] = mul(
                x[span, :], rot[0, :, first:first + TILE]
            ).astype(bf16)
            return 0
        lax.fori_loop(0, rows // TILE, body, 0)

    turn_right(half)
    core_wait(l_part, l_peer, l_core, 2)
    l_sum.send_near()
    a_sum[1].send_near()
    turn_right(half + TILE)

    ring_terms(pair, half, flip_r, b_part, b_peer, b_core)
    load_r[3].wait()

    def move_right(t, _):
        span = pl.ds(pl.multiple_of(t * TILE, TILE), TILE)
        moved[span, :] = mul(pair[span, half:], rot[1, half:, :])
        return 0

    lax.fori_loop(0, rows // TILE // 2, move_right, 0)
    a_sum[0].send_far()
    core_wait(b_part, b_peer, b_core, 2)
    b_sum.send_near()
    lax.fori_loop(rows // TILE // 2, rows // TILE, move_right, 0)
    a_sum[1].send_far()

    def move_left(t, _):
        span = pl.ds(pl.multiple_of(t * TILE, TILE), TILE)
        moved[span, :] += mul(pair[span, 0:TILE], rot[1, 0:TILE, :])
        return 0

    for q in range(CHUNKS):
        left_copy(q).wait_recv()
    for d in range(2):
        term = mul(flip_r[d * TILE:(d + 1) * TILE, :], pair[:, 0:TILE]).astype(bf16)
        c_part[0, d] = term[:LANE]
        c_part[1, d] = term[LANE:]
        core_copy(c_part, c_peer, c_core, d).start()
    lax.fori_loop(0, rows // TILE, move_left, 0)
    core_wait(c_part, c_peer, c_core, 2)
    l_sum.send_far()
    b_sum.send_far()
    c_sum.send_near()

    for q in range(CHUNKS):
        left_copy(CHUNKS + q).wait_recv()
    term = mul(flip_r[...], pair[:, column(2)]).astype(bf16)
    for i in range(4):
        d_part[i % 2, i // 2] = term[i * LANE:(i + 1) * LANE]
    core_send(d_part, d_peer, d_core, 2)

    edge = half // n

    def strip_rows(q):
        span = rows_of(q)
        left_copy(2 * CHUNKS + q).wait_recv()
        value = mul(flip_r[:, q * chunk:(q + 1) * chunk], pair[span, column(3)])
        if q > 0:
            value = value + strip[...]
        if q < CHUNKS - 1:
            strip[...] = value
        else:
            for i in range(n):
                h_part[i % 2, i // 2] = value[i * edge:(i + 1) * edge].astype(bf16)
            core_send(h_part, h_peer, h_core, 4)

    def move_rows(q):
        span = rows_of(q)
        value = moved[span, :] + mul(pair[span, TILE:half], rot[1, TILE:half, :])
        moved[span, :] = value
        return jnp.sum(value * value, axis=0, keepdims=True)

    strip_rows(0)
    squares = move_rows(0)
    core_wait(d_part, d_peer, d_core, 2)
    d_sum.send_near()

    def a_mirror_copy(k):
        return remote(
            a_turn.at[k - 1], a_turned.at[k - 1], a_mirror.at[0, k - 1], a_mirror.at[1, k - 1],
            me_col, lax.rem(me + k, n),
        )

    def l_mirror_copy():
        return remote(
            l_turn, l_turned, l_mirror.at[0], l_mirror.at[1], me_col, lax.rem(me + 1, 4)
        )

    def l_copy(col):
        return remote(l_row, l_in, l_sem.at[0], l_sem.at[1], col, me)

    def b_mirror_copy():
        return remote(
            b_turn, b_turned, b_mirror.at[0], b_mirror.at[1], me_col, 4 + lax.rem(me + 1, 4)
        )

    def c_mirror_copy(m, slot):
        return remote(
            c_turn.at[m], c_turned.at[slot], c_mirror_send.at[m], c_mirror_recv.at[slot],
            me_col, m,
        )

    def d_mirror_copy(slot):
        return remote(
            d_turn, d_turned.at[slot], d_mirror_send.at[0], d_mirror_recv.at[slot], me_col, 2
        )

    for q in range(1, CHUNKS - 1):
        strip_rows(q)
        squares = squares + move_rows(q)
    c_sum.send_far()
    d_sum.send_far()

    @pl.when(z < 2)
    def _():
        value = l_sum.total()
        l_turn[...] = value[:, LANE:2 * LANE].T.astype(bf16)
        l_mirror_copy().start()
        for k in range(3):
            l_row[:, column(lax.rem(me + k, 4))] = value[:, k * LANE:(k + 1) * LANE].astype(bf16)

    strip_rows(CHUNKS - 1)
    energy[...] = squares + move_rows(CHUNKS - 1)

    def e_copy(step):
        return remote(
            energy, energy_in.at[step - 1], e_sem.at[0, step - 1], e_sem.at[1, step - 1],
            me_col, lax.rem(me + step, n),
        )

    for step in range(1, n):
        e_copy(step).start()
    core_wait(h_part, h_peer, h_core, 4)
    h_sum.send()

    @pl.when(z < 2)
    def _():
        l_mirror_copy().wait_recv()
        l_row[:, column(lax.rem(me + 3, 4))] = l_turned[...]
        l_copy(following).start()

    for fly in a_sum:
        a_total[fly.span, :] = fly.total()
    for k in (3, 2, 1):
        a_turn[k - 1] = a_total[:, k * LANE:(k + 1) * LANE].T.astype(bf16)
        a_mirror_copy(k).start()
    for k in range(5):
        g1[:, column(lax.rem(me + k, n))] = a_total[:, k * LANE:(k + 1) * LANE]

    @pl.when(z >= 2)
    def _():
        value = b_sum.total()
        b_turn[...] = value[:, LANE:2 * LANE].T.astype(bf16)
        b_mirror_copy().start()
        for k in range(3):
            g2[:, column(4 + lax.rem(me + k, 4))] = value[:, k * LANE:(k + 1) * LANE]
        value = c_sum.total()
        g2[:, 0:TILE] = value
        for m in range(2):
            c_turn[m] = value[:, m * LANE:(m + 1) * LANE].T.astype(bf16)
            c_mirror_copy(m, me - 4).start()

    @pl.when(z >= 2)
    def _():
        value = d_sum.total()
        g2[:, column(2)] = value
        d_turn[...] = value.T.astype(bf16)
        d_mirror_copy(me - 4).start()


    total = energy[...]
    for step in range(1, n):
        e_copy(step).wait_recv()
        total = total + energy_in[step - 1]
    singular = jnp.sqrt(total * scale + 1e-06)
    factor = jnp.maximum(singular - 1.8, 0.0) / singular

    def shrink(t, _):
        span = pl.ds(pl.multiple_of(t * TILE, TILE), TILE)
        out[span, :] = (moved[span, :] * factor).astype(bf16)
        return 0

    lax.fori_loop(0, rows // TILE, shrink, 0)

    def h_row_copy(slot, row):
        return remote(h_out, h_row.at[slot], h_send.at[0], h_row_recv.at[slot], me_col, row)

    def h_col_copy(slot, row):
        place = slot * edge if isinstance(slot, int) else pl.multiple_of(slot * edge, edge)
        return remote(
            h_out, h_col.at[pl.ds(place, edge)], h_send.at[1], h_col_recv.at[slot], me_col, row
        )

    value = h_sum.total()
    h_out[...] = value.astype(bf16)

    @pl.when(me != 3)
    def _():
        h_col_copy(me, 3).start()

    @pl.when(me != 7)
    def _():
        h_row_copy(core, 4 + z).start()

    @pl.when(me == 3)
    def _():
        h_col[3 * edge:4 * edge, :] = value.astype(bf16)

    for k in (1, 2, 3):
        a_mirror_copy(k).wait_recv()
        g1[:, column(lax.rem(me + n - k, n))] = a_turned[k - 1].astype(f32)

    @pl.when(z >= 2)
    def _():
        b_mirror_copy().wait_recv()
        g2[:, column(4 + lax.rem(me + 3, 4))] = b_turned[...].astype(f32)

    @pl.when(z < 2)
    def _():
        l_copy(preceding).wait_recv()
        g2[:, 0:half] = l_in[...].astype(f32)

    @pl.when(z == 0)
    def _():
        for slot in range(4):
            remote(
                c_turn.at[0], c_turned.at[slot], c_mirror_send.at[0], c_mirror_recv.at[slot],
                me_col, partner,
            ).wait_recv()
            g2[:, column(4 + slot)] = c_turned[slot].astype(f32)

    @pl.when(me == 2)
    def _():
        for slot in range(4):
            remote(
                d_turn, d_turned.at[slot], d_mirror_send.at[0], d_mirror_recv.at[slot],
                me_col, partner,
            ).wait_recv()
            g2[:, column(4 + slot)] = d_turned[slot].astype(f32)

    @pl.when(z >= 2)
    def _():
        h_row_copy(0, partner).wait_recv()
        g2[0:edge, column(3)] = h_row[0].astype(f32)

    @pl.when((z >= 2) & (me != 7))
    def _():
        h_row_copy(1, partner).wait_recv()
        g2[edge:2 * edge, column(3)] = h_row[1].astype(f32)

    @pl.when(me == 7)
    def _():
        g2[edge:2 * edge, column(3)] = value

    @pl.when(me == 3)
    def _():
        for slot in range(n):
            if slot != 3:
                h_col_copy(slot, partner).wait_recv()
        for block in range(4):
            g2[:, column(4 + block)] = h_col[block * LANE:(block + 1) * LANE, :].T.astype(f32)

    for k in range(3 * CHUNKS):
        left_copy(k).wait_send()
    for part, peer, sems, count in (
        (a_part, a_peer, a_core, 4), (l_part, l_peer, l_core, 2), (b_part, b_peer, b_core, 2),
        (c_part, c_peer, c_core, 2), (d_part, d_peer, d_core, 2), (h_part, h_peer, h_core, 4),
    ):
        for d in range(count):
            core_copy(part, peer, sems, d).wait_send()
    for flow in (*a_sum, l_sum, b_sum, c_sum, d_sum, h_sum):
        flow.drain()
    for k in (1, 2, 3):
        a_mirror_copy(k).wait_send()

    @pl.when(z < 2)
    def _():
        l_mirror_copy().wait_send()
        l_copy(following).wait_send()

    @pl.when(z >= 2)
    def _():
        b_mirror_copy().wait_send()
        for m in range(2):
            c_mirror_copy(m, me - 4).wait_send()
        d_mirror_copy(me - 4).wait_send()

    @pl.when(me != 3)
    def _():
        h_col_copy(me, 3).wait_send()

    @pl.when(me != 7)
    def _():
        h_row_copy(core, 4 + z).wait_send()

    for step in range(1, n):
        e_copy(step).wait_send()


def general_kernel(
    n, n_col, x_hbm, rot_hbm, g1_hbm, g2_hbm, out_hbm,
    x, rot, left, pair, moved, part, peer, sums, landed,
    gram_out, energy, energy_in, shrunk,
    load_sem, left_send, left_recv, core_send, core_recv, z_send, z_recv,
    e_send, e_recv, store_sem, shrunk_sem,
):
    rows, width = x.shape
    half = width // 2
    block = width // n
    groups = n // 2
    total_rows = rows * n
    tiles = width // TILE
    row_tiles = rows // TILE
    per_tile = TILE // (2 * block)

    me_col = lax.axis_index("col")
    me = lax.axis_index("row")
    core = lax.rem(me, 2)
    group = lax.div(me, 2)
    partner = me + 1 - 2 * core

    def peer_at(step):
        return lax.rem(me + step, n)

    load_x = pltpu.make_async_copy(x_hbm, x, load_sem.at[0])
    load_r0 = [
        pltpu.make_async_copy(
            rot_hbm.at[0, :, pl.ds(h * half, half)], rot.at[0, :, pl.ds(h * half, half)],
            load_sem.at[1 + h],
        )
        for h in range(2)
    ]
    load_r1 = pltpu.make_async_copy(rot_hbm.at[1], rot.at[1], load_sem.at[3])
    load_x.start()
    load_r0[0].start()
    load_r0[1].start()
    load_r1.start()

    following = lax.rem(me_col + 1, n_col)
    preceding = lax.rem(me_col + n_col - 1, n_col)
    barrier = pltpu.get_barrier_semaphore()
    for other in (following, preceding):
        pl.semaphore_signal(
            barrier, inc=1, device_id={"col": other, "row": me},
            device_id_type=pl.DeviceIdType.MESH,
        )
    for step in range(1, n):
        pl.semaphore_signal(
            barrier, inc=1, device_id={"col": me_col, "row": peer_at(step)},
            device_id_type=pl.DeviceIdType.MESH,
        )

    def remote(src, dst, send_sem, recv_sem, col, row):
        return pltpu.make_async_remote_copy(
            src_ref=src, dst_ref=dst, send_sem=send_sem, recv_sem=recv_sem,
            device_id={"col": col, "row": row}, device_id_type=pl.DeviceIdType.MESH,
        )

    def turn(into, first, column):
        def body(t, _):
            span = pl.ds(pl.multiple_of(t * TILE, TILE), TILE)
            into[span, pl.ds(column - first, TILE)] = jnp.dot(
                x[span, :], rot[0, :, pl.ds(column, TILE)], preferred_element_type=jnp.float32
            ).astype(jnp.bfloat16)
            return 0
        lax.fori_loop(0, row_tiles, body, 0)

    pieces = half // TILE
    left_copy = [
        remote(
            left.at[:, pl.ds(h * TILE, TILE)], pair.at[:, pl.ds(h * TILE, TILE)],
            left_send.at[h], left_recv.at[h], following, me,
        )
        for h in range(pieces)
    ]
    load_x.wait()
    load_r0[0].wait()
    turn(left, 0, 0)
    pl.semaphore_wait(barrier, n + 1)
    left_copy[0].start()

    def z_copy(s, u):
        g = lax.rem(group + u, groups)
        k = lax.rem(g - group + 2 * groups - 1, groups)
        return remote(
            sums.at[s, g], landed.at[s, 0, k], z_send.at[s, k], z_recv.at[s, 0, k],
            me_col, 2 * g + core,
        )

    def added(s, u):
        return part[s, core, u].astype(jnp.float32) + peer[s, u].astype(jnp.float32)

    def rows_copy(s, q):
        span = pl.ds(q * per_tile, per_tile)
        return remote(
            part.at[s, 1 - core, span], peer.at[s, span],
            core_send.at[s, q], core_recv.at[s, q], me_col, partner,
        )

    def rows_terms(s, source):
        def body(q, _):
            turned_tile = source[:, pl.ds(pl.multiple_of(q * TILE, TILE), TILE)].T
            for m in range(tiles):
                term = jnp.dot(
                    turned_tile, source[:, m * TILE:(m + 1) * TILE],
                    preferred_element_type=jnp.float32,
                ).astype(jnp.bfloat16)
                for e in range(2 * per_tile):
                    part[s, e % 2, q * per_tile + e // 2, :, m * TILE:(m + 1) * TILE] = term[
                        e * block:(e + 1) * block, :
                    ]
            rows_copy(s, q).start()
            return 0
        lax.fori_loop(0, tiles, body, 0)

    def rows_pass(s):
        for q in range(tiles):
            rows_copy(s, q).wait_recv()

        def body(k, _):
            g = lax.rem(group + k, groups)
            sums[s, g] = added(s, g).astype(jnp.bfloat16)
            z_copy(s, k).start()
            return 0
        lax.fori_loop(1, groups, body, 0)

    def rows_sum(s):
        total = added(s, group)
        for k in range(1, groups):
            z_copy(s, k).wait_recv()
            total = total + landed[s, 0, k - 1].astype(jnp.float32)
        gram_out[s] = total / total_rows

    def gram_store(s, target):
        return pltpu.make_async_copy(gram_out.at[s], target, store_sem.at[s])

    rows_terms(0, x)
    for h in range(1, pieces):
        turn(left, 0, h * TILE)
        left_copy[h].start()
    rows_pass(0)
    load_r0[1].wait()
    for h in range(pieces):
        turn(pair, 0, half + h * TILE)
    load_r1.wait()

    def add_moved(first, depth, fresh):
        def body(t, acc):
            span = pl.ds(pl.multiple_of(t * TILE, TILE), TILE)
            value = jnp.dot(
                pair[span, pl.ds(first, depth)], rot[1, pl.ds(first, depth), :],
                preferred_element_type=jnp.float32,
            )
            if not fresh:
                value = value + moved[span, :]
            moved[span, :] = value
            return acc + jnp.sum(value * value, axis=0, keepdims=True)
        return lax.fori_loop(0, row_tiles, body, jnp.zeros((1, width), jnp.float32))

    add_moved(half, half, True)
    left_copy[0].wait_recv()
    for h in range(pieces - 1):
        if h > 0:
            left_copy[h].wait_recv()
        add_moved(h * TILE, TILE, False)
    rows_sum(0)
    gram_store(0, g1_hbm).start()
    left_copy[pieces - 1].wait_recv()
    rows_terms(1, pair)
    energy[...] = add_moved(half - TILE, TILE, False)

    def e_copy(step):
        return remote(
            energy, energy_in.at[step - 1], e_send.at[step - 1], e_recv.at[step - 1],
            me_col, peer_at(step),
        )

    for step in range(1, n):
        e_copy(step).start()
    rows_pass(1)
    total = energy[...]
    for step in range(1, n):
        e_copy(step).wait_recv()
        total = total + energy_in[step - 1]
    singular = jnp.sqrt(total / total_rows + 1e-06)
    factor = jnp.maximum(singular - 1.8, 0.0) / singular

    def out_copy(t):
        span = pl.ds(pl.multiple_of(t * TILE, TILE), TILE)
        return pltpu.make_async_copy(shrunk.at[span, :], out_hbm.at[span, :], shrunk_sem.at[t])

    def shrink(t, _):
        span = pl.ds(pl.multiple_of(t * TILE, TILE), TILE)
        shrunk[span, :] = (moved[span, :] * factor).astype(jnp.bfloat16)
        out_copy(t).start()
        return 0

    lax.fori_loop(0, row_tiles, shrink, 0)
    rows_sum(1)
    gram_store(1, g2_hbm).start()

    for h in range(pieces):
        left_copy[h].wait_send()
    for s in range(2):
        for q in range(tiles):
            rows_copy(s, q).wait_send()
        for k in range(1, groups):
            z_copy(s, k).wait_send()
    for step in range(1, n):
        e_copy(step).wait_send()
    for t in range(row_tiles):
        out_copy(t).wait()
    gram_store(0, g1_hbm).wait()
    gram_store(1, g2_hbm).wait()


def finish(*refs):
    sources, targets, sem = refs[:3], refs[3:6], refs[6]
    stores = [
        pltpu.make_async_copy(source, target, sem.at[at])
        for at, (source, target) in enumerate(zip(sources, targets))
    ]
    for store in stores:
        store.start()
    for store in stores:
        store.wait()


def general_scratch(n, rows, width):
    half = width // 2
    block = width // n
    groups = n // 2
    tiles = width // TILE
    sends = max(groups - 1, tiles)
    bf16, f32, dma = jnp.bfloat16, jnp.float32, pltpu.SemaphoreType.DMA
    return [
        pltpu.VMEM((rows, width), bf16),
        pltpu.VMEM((2, width, width), bf16),
        pltpu.VMEM((rows, half), bf16),
        pltpu.VMEM((rows, width), bf16),
        pltpu.VMEM((rows, width), f32),
        pltpu.VMEM((2, 2, groups, block, width), bf16),
        pltpu.VMEM((2, groups, block, width), bf16),
        pltpu.VMEM((2, groups, block, width), bf16),
        pltpu.VMEM((2, 1, groups - 1, block, width), bf16),
        pltpu.VMEM((2, block, width), f32),
        pltpu.VMEM((1, width), f32),
        pltpu.VMEM((n - 1, 1, width), f32),
        pltpu.VMEM((rows, width), bf16),
        dma((4,)),
        dma((half // TILE,)),
        dma((half // TILE,)),
        dma((2, sends)),
        dma((2, sends)),
        dma((2, sends)),
        dma((2, 1, groups - 1)),
        dma((n - 1,)),
        dma((n - 1,)),
        dma((2,)),
        dma((rows // TILE,)),
    ]


def paired_scratch(n, rows, width):
    half = width // 2
    bf16, f32, dma = jnp.bfloat16, jnp.float32, pltpu.SemaphoreType.DMA

    def room(*shape):
        return pltpu.VMEM(shape, bf16)

    return [
        room(rows, width),
        room(2, width, width),
        room(rows, half),
        room(rows, width),
        pltpu.VMEM((rows, width), f32),
        room(4, TILE, rows),
        room(half, rows),
        room(half, rows),
        pltpu.VMEM((half, LANE), f32),
        room(2, 4, LANE, 5 * LANE),
        room(4, LANE, 5 * LANE),
        room(4, LANE, 5 * LANE),
        room(2, LANE, 5 * LANE),
        room(LANE, 5 * LANE),
        pltpu.VMEM((LANE, 5 * LANE), f32),
        room(3, LANE, LANE),
        room(3, LANE, LANE),
        room(2, 2, LANE, 3 * LANE),
        room(2, LANE, 3 * LANE),
        room(2, LANE, 3 * LANE),
        room(2, LANE, 3 * LANE),
        room(LANE, 3 * LANE),
        room(LANE, LANE),
        room(LANE, LANE),
        room(LANE, half),
        room(LANE, half),
        room(2, 2, LANE, 3 * LANE),
        room(2, LANE, 3 * LANE),
        room(2, LANE, 3 * LANE),
        room(2, LANE, 3 * LANE),
        room(LANE, 3 * LANE),
        room(LANE, LANE),
        room(LANE, LANE),
        room(2, 2, LANE, TILE),
        room(2, LANE, TILE),
        room(2, LANE, TILE),
        room(2, LANE, TILE),
        room(LANE, TILE),
        room(2, LANE, LANE),
        room(4, LANE, LANE),
        room(2, 2, LANE, LANE),
        room(2, LANE, LANE),
        room(2, LANE, LANE),
        room(2, LANE, LANE),
        room(LANE, LANE),
        room(LANE, LANE),
        room(4, LANE, LANE),
        room(2, 4, half // n, LANE),
        room(4, half // n, LANE),
        room(4, half // n, LANE),
        room(3, half // n, LANE),
        room(half // n, LANE),
        room(2, half // n, LANE),
        room(half, LANE),
        pltpu.VMEM((1, width), f32),
        pltpu.VMEM((n - 1, 1, width), f32),
        dma((CHUNKS + 4,)),
        dma((3 * CHUNKS,)),
        dma((3 * CHUNKS,)),
        dma((2, 4)),
        dma((2, 4)),
        dma((2, 2)),
        dma((2, 3)),
        dma((2, 2)),
        dma((2, 2)),
        dma((2, 1)),
        dma((2,)),
        dma((2,)),
        dma((2, 2)),
        dma((2, 2)),
        dma((2, 1)),
        dma((2,)),
        dma((2, 2)),
        dma((2, 2)),
        dma((2, 1)),
        dma((2,)),
        dma((4,)),
        dma((2, 2)),
        dma((2, 2)),
        dma((2, 1)),
        dma((1,)),
        dma((4,)),
        dma((2, 4)),
        dma((2, 3)),
        dma((2,)),
        dma((2,)),
        dma((n,)),
        dma((2, n - 1)),
    ]


def per_device(n, n_col, snapshots, rotations):
    rows, width = snapshots.shape
    block = width // n
    paired = n == 8 and block == LANE and rows % (CHUNKS * TILE) == 0
    bf16, f32 = jnp.bfloat16, jnp.float32
    anywhere = pl.BlockSpec(memory_space=pl.ANY)
    inside = pl.BlockSpec(memory_space=pltpu.VMEM)
    shapes = (
        jax.ShapeDtypeStruct((block, width), f32),
        jax.ShapeDtypeStruct((block, width), f32),
        jax.ShapeDtypeStruct((rows, width), bf16),
    )
    if paired:
        body = functools.partial(paired_kernel, n_col)
    else:
        body = functools.partial(general_kernel, n, n_col)
    results = pl.pallas_call(
        body,
        out_shape=tuple(pltpu.VMEM(shape.shape, shape.dtype) for shape in shapes),
        in_specs=[anywhere] * 2,
        out_specs=(inside if paired else anywhere,) * 3,
        scratch_shapes=(paired_scratch if paired else general_scratch)(n, rows, width),
        compiler_params=pltpu.CompilerParams(
            collective_id=0, has_side_effects=True, vmem_limit_bytes=44 * 1024 * 1024
        ),
    )(*(pltpu.with_memory_space_constraint(a, pltpu.HBM) for a in (snapshots, rotations)))
    return pl.pallas_call(
        finish,
        out_shape=shapes,
        in_specs=[anywhere] * 3,
        out_specs=(anywhere,) * 3,
        scratch_shapes=[pltpu.SemaphoreType.DMA((3,))],
    )(*(pltpu.with_memory_space_constraint(r, pltpu.VMEM) for r in results))


def solution(mesh):
    return jax.shard_map(
        functools.partial(per_device, mesh.shape["row"], mesh.shape["col"]),
        mesh=mesh,
        in_specs=(P("row", "col"), P(None, "col", None)),
        out_specs=(P(("col", "row"), None), P(("col", "row"), None), P("row", "col")),
        check_vma=False,
    )
```

```python
import functools

import jax
import jax.numpy as jnp
from jax import lax
from jax.experimental import pallas as pl
from jax.experimental.pallas import tpu as pltpu
from jax.sharding import PartitionSpec as P

TILE = 256
LANE = 128
CHUNKS = 4


def paired_kernel(
    n_col, x_hbm, rot_hbm, g1, g2, out,
    x, rot, left, pair, moved, flip_x, flip_l, flip_r, strip,
    a_part, a_peer, a_sums, a_near, a_far, a_total, a_turn, a_turned,
    l_part, l_peer, l_sums, l_near, l_far, l_turn, l_turned, l_row, l_in,
    b_part, b_peer, b_sums, b_near, b_far, b_turn, b_turned,
    c_part, c_peer, c_sums, c_near, c_far, c_turn, c_turned,
    d_part, d_peer, d_sums, d_near, d_far, d_turn, d_turned,
    h_part, h_peer, h_sums, h_land, h_out, h_row, h_col,
    energy, energy_in,
    load_sem, left_send, left_recv, a_core, a_first, a_second, a_mirror,
    l_core, l_first, l_second, l_mirror, l_sem,
    b_core, b_first, b_second, b_mirror,
    c_core, c_first, c_second, c_mirror_send, c_mirror_recv,
    d_core, d_first, d_second, d_mirror_send, d_mirror_recv,
    h_core, h_z, h_send, h_row_recv, h_col_recv, e_sem,
):
    n = 8
    rows, width = x.shape
    half = width // 2
    scale = 1.0 / (rows * n)
    chunk = rows // CHUNKS
    f32, bf16 = jnp.float32, jnp.bfloat16

    me_col = lax.axis_index("col")
    me = lax.axis_index("row")
    core = lax.rem(me, 2)
    z = lax.div(me, 2)
    partner = me + 1 - 2 * core
    beside = z + 1 - 2 * lax.rem(z, 2)
    across = 3 - z
    opposite = lax.rem(z + 2, 4)
    following = lax.rem(me_col + 1, n_col)
    preceding = lax.rem(me_col + n_col - 1, n_col)

    def rows_of(q):
        return pl.ds(q * chunk, chunk)

    def load(source, target, at):
        return pltpu.make_async_copy(source, target, load_sem.at[at])

    load_x = [load(x_hbm.at[rows_of(q)], x.at[rows_of(q)], q) for q in range(CHUNKS)]
    parts = ((0, 0, TILE), (0, TILE, TILE), (0, half, half), (1, 0, width))
    load_r = [
        load(
            rot_hbm.at[s, :, pl.ds(first, size)], rot.at[s, :, pl.ds(first, size)], CHUNKS + k
        )
        for k, (s, first, size) in enumerate(parts)
    ]
    barrier = pltpu.get_barrier_semaphore()
    for other in (following, preceding):
        pl.semaphore_signal(
            barrier, inc=1, device_id={"col": other, "row": me},
            device_id_type=pl.DeviceIdType.MESH,
        )
    for step in range(1, n):
        pl.semaphore_signal(
            barrier, inc=1, device_id={"col": me_col, "row": lax.rem(me + step, n)},
            device_id_type=pl.DeviceIdType.MESH,
        )

    load_x[0].start()
    load_r[0].start()
    for q in range(1, CHUNKS):
        load_x[q].start()
    for k in range(1, 4):
        load_r[k].start()

    def remote(src, dst, send_sem, recv_sem, col, row):
        return pltpu.make_async_remote_copy(
            src_ref=src, dst_ref=dst, send_sem=send_sem, recv_sem=recv_sem,
            device_id={"col": col, "row": row}, device_id_type=pl.DeviceIdType.MESH,
        )

    def to_chip(src, dst, sems, at, chip):
        return remote(src, dst, sems.at[0, at], sems.at[1, at], me_col, 2 * chip + core)

    def mul(a, b):
        return jnp.dot(a, b, preferred_element_type=f32)

    def when(condition, run):
        if condition is True:
            run()
        else:
            pl.when(condition)(run)

    def left_copy(k):
        q = k % CHUNKS
        first, size = ((0, TILE), (TILE, LANE), (TILE + LANE, LANE))[k // CHUNKS]
        here = (rows_of(q), pl.ds(first, size))
        return remote(
            left.at[here], pair.at[here], left_send.at[k], left_recv.at[k], following, me
        )

    load_r[0].wait()
    for q in range(CHUNKS):
        load_x[q].wait()
        left[rows_of(q), 0:TILE] = mul(x[rows_of(q), :], rot[0, :, 0:TILE]).astype(bf16)
        if q == 0:
            pl.semaphore_wait(barrier, n + 1)
        left_copy(q).start()

    def core_copy(part, peer, sems, at):
        return remote(
            part.at[1 - core, at], peer.at[at], sems.at[0, at], sems.at[1, at], me_col, partner
        )

    def added(part, peer, at, span):
        return part[core, at, span, :].astype(f32) + peer[at, span, :].astype(f32)

    class Fly:
        def __init__(self, part, peer, sums, near, far, near_sems, far_sems, base, span, first, second,
                     shift=0, live=lambda d: True):
            self.part, self.peer, self.sums, self.near, self.far = part, peer, sums, near, far
            self.near_sems, self.far_sems, self.base, self.span = near_sems, far_sems, base, span
            self.first, self.second, self.shift, self.live = first, second, shift, live

        def near_copy(self, slot, d):
            return to_chip(
                self.sums.at[d - self.shift, self.span], self.near.at[slot, self.span],
                self.near_sems, 2 * self.base + slot, self.first,
            )

        def far_copy(self):
            return to_chip(
                self.sums.at[self.second - self.shift, self.span], self.far.at[self.span],
                self.far_sems, self.base, self.second,
            )

        def term(self, d):
            return added(self.part, self.peer, d - self.shift, self.span)

        def send_near(self):
            for slot, d in enumerate((self.first, opposite)):
                def run(slot=slot, d=d):
                    self.sums[d - self.shift, self.span, :] = self.term(d).astype(bf16)
                    self.near_copy(slot, d).start()
                when(self.live(d), run)

        def send_far(self):
            def run():
                d = self.second
                self.near_copy(1, d).wait_recv()
                self.sums[d - self.shift, self.span, :] = (
                    self.term(d) + self.near[1, self.span, :].astype(f32)
                ).astype(bf16)
                self.far_copy().start()
            when(self.live(self.second), run)

        def total(self):
            self.near_copy(0, z).wait_recv()
            to_chip(
                self.sums.at[z - self.shift, self.span], self.far.at[self.span],
                self.far_sems, self.base, self.second,
            ).wait_recv()
            return (
                self.term(z) + self.near[0, self.span, :].astype(f32)
                + self.far[self.span, :].astype(f32)
            ) * scale

        def drain(self):
            for slot, d in enumerate((self.first, opposite)):
                when(self.live(d), lambda slot=slot, d=d: self.near_copy(slot, d).wait_send())
            when(self.live(self.second), lambda: self.far_copy().wait_send())

    everything = pl.ds(0, LANE)
    upper, lower = pl.ds(0, LANE // 2), pl.ds(LANE // 2, LANE // 2)
    a_sum = (
        Fly(a_part, a_peer, a_sums, a_near, a_far, a_first, a_second, 0, upper, beside, across),
        Fly(a_part, a_peer, a_sums, a_near, a_far, a_first, a_second, 1, lower, beside, across),
    )
    b_sum = Fly(
        b_part, b_peer, b_sums, b_near, b_far, b_first, b_second, 0, everything, beside, across,
        shift=2, live=lambda d: d >= 2,
    )

    class Direct:
        def __init__(self, part, peer, sums, land, sems):
            self.part, self.peer, self.sums, self.land, self.sems = part, peer, sums, land, sems

        def copy(self, slot, source, chip):
            return to_chip(self.sums.at[source], self.land.at[slot], self.sems, slot, chip)

        def send(self):
            for slot, d in enumerate((opposite, across, beside)):
                self.sums[d] = added(self.part, self.peer, d, slice(None)).astype(bf16)
                self.copy(slot, d, d).start()

        def total(self):
            value = added(self.part, self.peer, z, slice(None))
            for slot, d in ((2, beside), (1, across), (0, opposite)):
                self.copy(slot, z, d).wait_recv()
                value = value + self.land[slot].astype(f32)
            return value * scale

        def drain(self):
            for slot, d in enumerate((opposite, across, beside)):
                self.copy(slot, d, d).wait_send()

    l_sum = Fly(
        l_part, l_peer, l_sums, l_near, l_far, l_first, l_second, 0, everything, beside, across,
        live=lambda d: d < 2,
    )
    c_sum = Fly(
        c_part, c_peer, c_sums, c_near, c_far, c_first, c_second, 0, everything, beside, across,
        shift=2, live=lambda d: d >= 2,
    )
    d_sum = Fly(
        d_part, d_peer, d_sums, d_near, d_far, d_first, d_second, 0, everything, beside, across,
        shift=2, live=lambda d: d >= 2,
    )
    h_sum = Direct(h_part, h_peer, h_sums, h_land, h_z)

    def column(block):
        if isinstance(block, int):
            return pl.ds(block * LANE, LANE)
        return pl.ds(pl.multiple_of(block * LANE, LANE), LANE)

    for d in range(4):
        flip_x[d] = x[:, d * TILE:(d + 1) * TILE].T
        for k in range(3):
            m = (d + k) % 4
            term = mul(flip_x[d], x[:, m * TILE:(m + 1) * TILE]).astype(bf16)
            for e in range(2):
                for b in range(2):
                    slot = 2 * k + b - e
                    if 0 <= slot <= 4:
                        a_part[e, d, :, slot * LANE:(slot + 1) * LANE] = term[
                            e * LANE:(e + 1) * LANE, b * LANE:(b + 1) * LANE
                        ]
        core_copy(a_part, a_peer, a_core, d).start()

    load_r[1].wait()
    for q in range(CHUNKS):
        left[rows_of(q), TILE:half] = mul(x[rows_of(q), :], rot[0, :, TILE:half]).astype(bf16)
        left_copy(CHUNKS + q).start()
    for q in range(CHUNKS):
        left_copy(2 * CHUNKS + q).start()

    for d in range(4):
        core_copy(a_part, a_peer, a_core, d).wait_recv()
    a_sum[0].send_near()
    def core_send(part, peer, sems, count):
        for d in range(count):
            core_copy(part, peer, sems, d).start()

    def core_wait(part, peer, sems, count):
        for d in range(count):
            core_copy(part, peer, sems, d).wait_recv()

    def ring_terms(source, first, flip, part, peer, sems):
        for d in range(2):
            flip[d * TILE:(d + 1) * TILE, :] = source[
                :, first + d * TILE:first + (d + 1) * TILE
            ].T
            term = mul(flip[d * TILE:(d + 1) * TILE, :], source[:, first:first + half]).astype(bf16)
            for e in range(2):
                for k in range(3):
                    at = (2 * d + e + k) % 4 * LANE
                    part[e, d, :, k * LANE:(k + 1) * LANE] = term[
                        e * LANE:(e + 1) * LANE, at:at + LANE
                    ]
            core_copy(part, peer, sems, d).start()

    ring_terms(left, 0, flip_l, l_part, l_peer, l_core)
    load_r[2].wait()

    def turn_right(first):
        def body(t, _):
            span = pl.ds(pl.multiple_of(t * TILE, TILE), TILE)
            pair[span, first:first + TILE] = mul(
                x[span, :], rot[0, :, first:first + TILE]
            ).astype(bf16)
            return 0
        lax.fori_loop(0, rows // TILE, body, 0)

    turn_right(half)
    core_wait(l_part, l_peer, l_core, 2)
    l_sum.send_near()
    a_sum[1].send_near()
    turn_right(half + TILE)

    ring_terms(pair, half, flip_r, b_part, b_peer, b_core)
    load_r[3].wait()

    def move_right(t, _):
        span = pl.ds(pl.multiple_of(t * TILE, TILE), TILE)
        moved[span, :] = mul(pair[span, half:], rot[1, half:, :])
        return 0

    lax.fori_loop(0, rows // TILE // 2, move_right, 0)
    a_sum[0].send_far()
    core_wait(b_part, b_peer, b_core, 2)
    b_sum.send_near()
    lax.fori_loop(rows // TILE // 2, rows // TILE, move_right, 0)
    a_sum[1].send_far()

    def move_left(t, _):
        span = pl.ds(pl.multiple_of(t * TILE, TILE), TILE)
        moved[span, :] += mul(pair[span, 0:TILE], rot[1, 0:TILE, :])
        return 0

    for q in range(CHUNKS):
        left_copy(q).wait_recv()
    for d in range(2):
        term = mul(flip_r[d * TILE:(d + 1) * TILE, :], pair[:, 0:TILE]).astype(bf16)
        c_part[0, d] = term[:LANE]
        c_part[1, d] = term[LANE:]
        core_copy(c_part, c_peer, c_core, d).start()
    lax.fori_loop(0, rows // TILE, move_left, 0)
    core_wait(c_part, c_peer, c_core, 2)
    l_sum.send_far()
    b_sum.send_far()
    c_sum.send_near()

    for q in range(CHUNKS):
        left_copy(CHUNKS + q).wait_recv()
    term = mul(flip_r[...], pair[:, column(2)]).astype(bf16)
    for i in range(4):
        d_part[i % 2, i // 2] = term[i * LANE:(i + 1) * LANE]
    core_send(d_part, d_peer, d_core, 2)

    edge = half // n

    def strip_rows(q):
        span = rows_of(q)
        left_copy(2 * CHUNKS + q).wait_recv()
        value = mul(flip_r[:, q * chunk:(q + 1) * chunk], pair[span, column(3)])
        if q > 0:
            value = value + strip[...]
        if q < CHUNKS - 1:
            strip[...] = value
        else:
            for i in range(n):
                h_part[i % 2, i // 2] = value[i * edge:(i + 1) * edge].astype(bf16)
            core_send(h_part, h_peer, h_core, 4)

    def move_rows(q):
        span = rows_of(q)
        value = moved[span, :] + mul(pair[span, TILE:half], rot[1, TILE:half, :])
        moved[span, :] = value
        return jnp.sum(value * value, axis=0, keepdims=True)

    strip_rows(0)
    squares = move_rows(0)
    core_wait(d_part, d_peer, d_core, 2)
    d_sum.send_near()

    def a_mirror_copy(k):
        return remote(
            a_turn.at[k - 1], a_turned.at[k - 1], a_mirror.at[0, k - 1], a_mirror.at[1, k - 1],
            me_col, lax.rem(me + k, n),
        )

    def l_mirror_copy():
        return remote(
            l_turn, l_turned, l_mirror.at[0], l_mirror.at[1], me_col, lax.rem(me + 1, 4)
        )

    def l_copy(col):
        return remote(l_row, l_in, l_sem.at[0], l_sem.at[1], col, me)

    def b_mirror_copy():
        return remote(
            b_turn, b_turned, b_mirror.at[0], b_mirror.at[1], me_col, 4 + lax.rem(me + 1, 4)
        )

    def c_mirror_copy(m, slot):
        return remote(
            c_turn.at[m], c_turned.at[slot], c_mirror_send.at[m], c_mirror_recv.at[slot],
            me_col, m,
        )

    def d_mirror_copy(slot):
        return remote(
            d_turn, d_turned.at[slot], d_mirror_send.at[0], d_mirror_recv.at[slot], me_col, 2
        )

    for q in range(1, CHUNKS - 1):
        strip_rows(q)
        squares = squares + move_rows(q)
    c_sum.send_far()
    d_sum.send_far()

    @pl.when(z < 2)
    def _():
        value = l_sum.total()
        l_turn[...] = value[:, LANE:2 * LANE].T.astype(bf16)
        l_mirror_copy().start()
        for k in range(3):
            l_row[:, column(lax.rem(me + k, 4))] = value[:, k * LANE:(k + 1) * LANE].astype(bf16)

    strip_rows(CHUNKS - 1)
    energy[...] = squares + move_rows(CHUNKS - 1)

    def e_copy(step):
        return remote(
            energy, energy_in.at[step - 1], e_sem.at[0, step - 1], e_sem.at[1, step - 1],
            me_col, lax.rem(me + step, n),
        )

    core_wait(h_part, h_peer, h_core, 4)
    h_sum.send()
    for step in range(1, n):
        e_copy(step).start()

    @pl.when(z < 2)
    def _():
        l_mirror_copy().wait_recv()
        l_row[:, column(lax.rem(me + 3, 4))] = l_turned[...]
        l_copy(following).start()

    for fly in a_sum:
        a_total[fly.span, :] = fly.total()
    for k in (3, 2, 1):
        a_turn[k - 1] = a_total[:, k * LANE:(k + 1) * LANE].T.astype(bf16)
        a_mirror_copy(k).start()
    for k in range(5):
        g1[:, column(lax.rem(me + k, n))] = a_total[:, k * LANE:(k + 1) * LANE]

    @pl.when(z >= 2)
    def _():
        value = b_sum.total()
        b_turn[...] = value[:, LANE:2 * LANE].T.astype(bf16)
        b_mirror_copy().start()
        for k in range(3):
            g2[:, column(4 + lax.rem(me + k, 4))] = value[:, k * LANE:(k + 1) * LANE]
        value = c_sum.total()
        g2[:, 0:TILE] = value
        for m in range(2):
            c_turn[m] = value[:, m * LANE:(m + 1) * LANE].T.astype(bf16)
            c_mirror_copy(m, me - 4).start()

    @pl.when(z >= 2)
    def _():
        value = d_sum.total()
        g2[:, column(2)] = value
        d_turn[...] = value.T.astype(bf16)
        d_mirror_copy(me - 4).start()


    total = energy[...]
    for step in range(1, n):
        e_copy(step).wait_recv()
        total = total + energy_in[step - 1]
    singular = jnp.sqrt(total * scale + 1e-06)
    factor = jnp.maximum(singular - 1.8, 0.0) / singular

    def shrink(t, _):
        span = pl.ds(pl.multiple_of(t * TILE, TILE), TILE)
        out[span, :] = (moved[span, :] * factor).astype(bf16)
        return 0

    lax.fori_loop(0, rows // TILE, shrink, 0)

    def h_row_copy(slot, row):
        return remote(h_out, h_row.at[slot], h_send.at[0], h_row_recv.at[slot], me_col, row)

    def h_col_copy(slot, row):
        place = slot * edge if isinstance(slot, int) else pl.multiple_of(slot * edge, edge)
        return remote(
            h_out, h_col.at[pl.ds(place, edge)], h_send.at[1], h_col_recv.at[slot], me_col, row
        )

    value = h_sum.total()
    h_out[...] = value.astype(bf16)

    @pl.when(me != 3)
    def _():
        h_col_copy(me, 3).start()

    @pl.when(me != 7)
    def _():
        h_row_copy(core, 4 + z).start()

    @pl.when(me == 3)
    def _():
        h_col[3 * edge:4 * edge, :] = value.astype(bf16)

    for k in (1, 2, 3):
        a_mirror_copy(k).wait_recv()
        g1[:, column(lax.rem(me + n - k, n))] = a_turned[k - 1].astype(f32)

    @pl.when(z >= 2)
    def _():
        b_mirror_copy().wait_recv()
        g2[:, column(4 + lax.rem(me + 3, 4))] = b_turned[...].astype(f32)

    @pl.when(z < 2)
    def _():
        l_copy(preceding).wait_recv()
        g2[:, 0:half] = l_in[...].astype(f32)

    @pl.when(z == 0)
    def _():
        for slot in range(4):
            remote(
                c_turn.at[0], c_turned.at[slot], c_mirror_send.at[0], c_mirror_recv.at[slot],
                me_col, partner,
            ).wait_recv()
            g2[:, column(4 + slot)] = c_turned[slot].astype(f32)

    @pl.when(me == 2)
    def _():
        for slot in range(4):
            remote(
                d_turn, d_turned.at[slot], d_mirror_send.at[0], d_mirror_recv.at[slot],
                me_col, partner,
            ).wait_recv()
            g2[:, column(4 + slot)] = d_turned[slot].astype(f32)

    @pl.when(z >= 2)
    def _():
        h_row_copy(0, partner).wait_recv()
        g2[0:edge, column(3)] = h_row[0].astype(f32)

    @pl.when((z >= 2) & (me != 7))
    def _():
        h_row_copy(1, partner).wait_recv()
        g2[edge:2 * edge, column(3)] = h_row[1].astype(f32)

    @pl.when(me == 7)
    def _():
        g2[edge:2 * edge, column(3)] = value

    @pl.when(me == 3)
    def _():
        for slot in range(n):
            if slot != 3:
                h_col_copy(slot, partner).wait_recv()
        for block in range(4):
            g2[:, column(4 + block)] = h_col[block * LANE:(block + 1) * LANE, :].T.astype(f32)

    for k in range(3 * CHUNKS):
        left_copy(k).wait_send()
    for part, peer, sems, count in (
        (a_part, a_peer, a_core, 4), (l_part, l_peer, l_core, 2), (b_part, b_peer, b_core, 2),
        (c_part, c_peer, c_core, 2), (d_part, d_peer, d_core, 2), (h_part, h_peer, h_core, 4),
    ):
        for d in range(count):
            core_copy(part, peer, sems, d).wait_send()
    for flow in (*a_sum, l_sum, b_sum, c_sum, d_sum, h_sum):
        flow.drain()
    for k in (1, 2, 3):
        a_mirror_copy(k).wait_send()

    @pl.when(z < 2)
    def _():
        l_mirror_copy().wait_send()
        l_copy(following).wait_send()

    @pl.when(z >= 2)
    def _():
        b_mirror_copy().wait_send()
        for m in range(2):
            c_mirror_copy(m, me - 4).wait_send()
        d_mirror_copy(me - 4).wait_send()

    @pl.when(me != 3)
    def _():
        h_col_copy(me, 3).wait_send()

    @pl.when(me != 7)
    def _():
        h_row_copy(core, 4 + z).wait_send()

    for step in range(1, n):
        e_copy(step).wait_send()


def general_kernel(
    n, n_col, x_hbm, rot_hbm, g1_hbm, g2_hbm, out_hbm,
    x, rot, left, pair, moved, part, peer, sums, landed,
    gram_out, energy, energy_in, shrunk,
    load_sem, left_send, left_recv, core_send, core_recv, z_send, z_recv,
    e_send, e_recv, store_sem, shrunk_sem,
):
    rows, width = x.shape
    half = width // 2
    block = width // n
    groups = n // 2
    total_rows = rows * n
    tiles = width // TILE
    row_tiles = rows // TILE
    per_tile = TILE // (2 * block)

    me_col = lax.axis_index("col")
    me = lax.axis_index("row")
    core = lax.rem(me, 2)
    group = lax.div(me, 2)
    partner = me + 1 - 2 * core

    def peer_at(step):
        return lax.rem(me + step, n)

    load_x = pltpu.make_async_copy(x_hbm, x, load_sem.at[0])
    load_r0 = [
        pltpu.make_async_copy(
            rot_hbm.at[0, :, pl.ds(h * half, half)], rot.at[0, :, pl.ds(h * half, half)],
            load_sem.at[1 + h],
        )
        for h in range(2)
    ]
    load_r1 = pltpu.make_async_copy(rot_hbm.at[1], rot.at[1], load_sem.at[3])
    load_x.start()
    load_r0[0].start()
    load_r0[1].start()
    load_r1.start()

    following = lax.rem(me_col + 1, n_col)
    preceding = lax.rem(me_col + n_col - 1, n_col)
    barrier = pltpu.get_barrier_semaphore()
    for other in (following, preceding):
        pl.semaphore_signal(
            barrier, inc=1, device_id={"col": other, "row": me},
            device_id_type=pl.DeviceIdType.MESH,
        )
    for step in range(1, n):
        pl.semaphore_signal(
            barrier, inc=1, device_id={"col": me_col, "row": peer_at(step)},
            device_id_type=pl.DeviceIdType.MESH,
        )

    def remote(src, dst, send_sem, recv_sem, col, row):
        return pltpu.make_async_remote_copy(
            src_ref=src, dst_ref=dst, send_sem=send_sem, recv_sem=recv_sem,
            device_id={"col": col, "row": row}, device_id_type=pl.DeviceIdType.MESH,
        )

    def turn(into, first, column):
        def body(t, _):
            span = pl.ds(pl.multiple_of(t * TILE, TILE), TILE)
            into[span, pl.ds(column - first, TILE)] = jnp.dot(
                x[span, :], rot[0, :, pl.ds(column, TILE)], preferred_element_type=jnp.float32
            ).astype(jnp.bfloat16)
            return 0
        lax.fori_loop(0, row_tiles, body, 0)

    pieces = half // TILE
    left_copy = [
        remote(
            left.at[:, pl.ds(h * TILE, TILE)], pair.at[:, pl.ds(h * TILE, TILE)],
            left_send.at[h], left_recv.at[h], following, me,
        )
        for h in range(pieces)
    ]
    load_x.wait()
    load_r0[0].wait()
    turn(left, 0, 0)
    pl.semaphore_wait(barrier, n + 1)
    left_copy[0].start()

    def z_copy(s, u):
        g = lax.rem(group + u, groups)
        k = lax.rem(g - group + 2 * groups - 1, groups)
        return remote(
            sums.at[s, g], landed.at[s, 0, k], z_send.at[s, k], z_recv.at[s, 0, k],
            me_col, 2 * g + core,
        )

    def added(s, u):
        return part[s, core, u].astype(jnp.float32) + peer[s, u].astype(jnp.float32)

    def rows_copy(s, q):
        span = pl.ds(q * per_tile, per_tile)
        return remote(
            part.at[s, 1 - core, span], peer.at[s, span],
            core_send.at[s, q], core_recv.at[s, q], me_col, partner,
        )

    def rows_terms(s, source):
        def body(q, _):
            turned_tile = source[:, pl.ds(pl.multiple_of(q * TILE, TILE), TILE)].T
            for m in range(tiles):
                term = jnp.dot(
                    turned_tile, source[:, m * TILE:(m + 1) * TILE],
                    preferred_element_type=jnp.float32,
                ).astype(jnp.bfloat16)
                for e in range(2 * per_tile):
                    part[s, e % 2, q * per_tile + e // 2, :, m * TILE:(m + 1) * TILE] = term[
                        e * block:(e + 1) * block, :
                    ]
            rows_copy(s, q).start()
            return 0
        lax.fori_loop(0, tiles, body, 0)

    def rows_pass(s):
        for q in range(tiles):
            rows_copy(s, q).wait_recv()

        def body(k, _):
            g = lax.rem(group + k, groups)
            sums[s, g] = added(s, g).astype(jnp.bfloat16)
            z_copy(s, k).start()
            return 0
        lax.fori_loop(1, groups, body, 0)

    def rows_sum(s):
        total = added(s, group)
        for k in range(1, groups):
            z_copy(s, k).wait_recv()
            total = total + landed[s, 0, k - 1].astype(jnp.float32)
        gram_out[s] = total / total_rows

    def gram_store(s, target):
        return pltpu.make_async_copy(gram_out.at[s], target, store_sem.at[s])

    rows_terms(0, x)
    for h in range(1, pieces):
        turn(left, 0, h * TILE)
        left_copy[h].start()
    rows_pass(0)
    load_r0[1].wait()
    for h in range(pieces):
        turn(pair, 0, half + h * TILE)
    load_r1.wait()

    def add_moved(first, depth, fresh):
        def body(t, acc):
            span = pl.ds(pl.multiple_of(t * TILE, TILE), TILE)
            value = jnp.dot(
                pair[span, pl.ds(first, depth)], rot[1, pl.ds(first, depth), :],
                preferred_element_type=jnp.float32,
            )
            if not fresh:
                value = value + moved[span, :]
            moved[span, :] = value
            return acc + jnp.sum(value * value, axis=0, keepdims=True)
        return lax.fori_loop(0, row_tiles, body, jnp.zeros((1, width), jnp.float32))

    add_moved(half, half, True)
    left_copy[0].wait_recv()
    for h in range(pieces - 1):
        if h > 0:
            left_copy[h].wait_recv()
        add_moved(h * TILE, TILE, False)
    rows_sum(0)
    gram_store(0, g1_hbm).start()
    left_copy[pieces - 1].wait_recv()
    rows_terms(1, pair)
    energy[...] = add_moved(half - TILE, TILE, False)

    def e_copy(step):
        return remote(
            energy, energy_in.at[step - 1], e_send.at[step - 1], e_recv.at[step - 1],
            me_col, peer_at(step),
        )

    rows_pass(1)
    total = energy[...]
    for step in range(1, n):
        e_copy(step).wait_recv()
        total = total + energy_in[step - 1]
    singular = jnp.sqrt(total / total_rows + 1e-06)
    factor = jnp.maximum(singular - 1.8, 0.0) / singular

    def out_copy(t):
        span = pl.ds(pl.multiple_of(t * TILE, TILE), TILE)
        return pltpu.make_async_copy(shrunk.at[span, :], out_hbm.at[span, :], shrunk_sem.at[t])

    def shrink(t, _):
        span = pl.ds(pl.multiple_of(t * TILE, TILE), TILE)
        shrunk[span, :] = (moved[span, :] * factor).astype(jnp.bfloat16)
        out_copy(t).start()
        return 0

    lax.fori_loop(0, row_tiles, shrink, 0)
    rows_sum(1)
    gram_store(1, g2_hbm).start()

    for h in range(pieces):
        left_copy[h].wait_send()
    for s in range(2):
        for q in range(tiles):
            rows_copy(s, q).wait_send()
        for k in range(1, groups):
            z_copy(s, k).wait_send()
    for step in range(1, n):
        e_copy(step).wait_send()
    for t in range(row_tiles):
        out_copy(t).wait()
    gram_store(0, g1_hbm).wait()
    gram_store(1, g2_hbm).wait()


def finish(*refs):
    sources, targets, sem = refs[:3], refs[3:6], refs[6]
    stores = [
        pltpu.make_async_copy(source, target, sem.at[at])
        for at, (source, target) in enumerate(zip(sources, targets))
    ]
    for store in stores:
        store.start()
    for store in stores:
        store.wait()


def general_scratch(n, rows, width):
    half = width // 2
    block = width // n
    groups = n // 2
    tiles = width // TILE
    sends = max(groups - 1, tiles)
    bf16, f32, dma = jnp.bfloat16, jnp.float32, pltpu.SemaphoreType.DMA
    return [
        pltpu.VMEM((rows, width), bf16),
        pltpu.VMEM((2, width, width), bf16),
        pltpu.VMEM((rows, half), bf16),
        pltpu.VMEM((rows, width), bf16),
        pltpu.VMEM((rows, width), f32),
        pltpu.VMEM((2, 2, groups, block, width), bf16),
        pltpu.VMEM((2, groups, block, width), bf16),
        pltpu.VMEM((2, groups, block, width), bf16),
        pltpu.VMEM((2, 1, groups - 1, block, width), bf16),
        pltpu.VMEM((2, block, width), f32),
        pltpu.VMEM((1, width), f32),
        pltpu.VMEM((n - 1, 1, width), f32),
        pltpu.VMEM((rows, width), bf16),
        dma((4,)),
        dma((half // TILE,)),
        dma((half // TILE,)),
        dma((2, sends)),
        dma((2, sends)),
        dma((2, sends)),
        dma((2, 1, groups - 1)),
        dma((n - 1,)),
        dma((n - 1,)),
        dma((2,)),
        dma((rows // TILE,)),
    ]


def paired_scratch(n, rows, width):
    half = width // 2
    bf16, f32, dma = jnp.bfloat16, jnp.float32, pltpu.SemaphoreType.DMA

    def room(*shape):
        return pltpu.VMEM(shape, bf16)

    return [
        room(rows, width),
        room(2, width, width),
        room(rows, half),
        room(rows, width),
        pltpu.VMEM((rows, width), f32),
        room(4, TILE, rows),
        room(half, rows),
        room(half, rows),
        pltpu.VMEM((half, LANE), f32),
        room(2, 4, LANE, 5 * LANE),
        room(4, LANE, 5 * LANE),
        room(4, LANE, 5 * LANE),
        room(2, LANE, 5 * LANE),
        room(LANE, 5 * LANE),
        pltpu.VMEM((LANE, 5 * LANE), f32),
        room(3, LANE, LANE),
        room(3, LANE, LANE),
        room(2, 2, LANE, 3 * LANE),
        room(2, LANE, 3 * LANE),
        room(2, LANE, 3 * LANE),
        room(2, LANE, 3 * LANE),
        room(LANE, 3 * LANE),
        room(LANE, LANE),
        room(LANE, LANE),
        room(LANE, half),
        room(LANE, half),
        room(2, 2, LANE, 3 * LANE),
        room(2, LANE, 3 * LANE),
        room(2, LANE, 3 * LANE),
        room(2, LANE, 3 * LANE),
        room(LANE, 3 * LANE),
        room(LANE, LANE),
        room(LANE, LANE),
        room(2, 2, LANE, TILE),
        room(2, LANE, TILE),
        room(2, LANE, TILE),
        room(2, LANE, TILE),
        room(LANE, TILE),
        room(2, LANE, LANE),
        room(4, LANE, LANE),
        room(2, 2, LANE, LANE),
        room(2, LANE, LANE),
        room(2, LANE, LANE),
        room(2, LANE, LANE),
        room(LANE, LANE),
        room(LANE, LANE),
        room(4, LANE, LANE),
        room(2, 4, half // n, LANE),
        room(4, half // n, LANE),
        room(4, half // n, LANE),
        room(3, half // n, LANE),
        room(half // n, LANE),
        room(2, half // n, LANE),
        room(half, LANE),
        pltpu.VMEM((1, width), f32),
        pltpu.VMEM((n - 1, 1, width), f32),
        dma((CHUNKS + 4,)),
        dma((3 * CHUNKS,)),
        dma((3 * CHUNKS,)),
        dma((2, 4)),
        dma((2, 4)),
        dma((2, 2)),
        dma((2, 3)),
        dma((2, 2)),
        dma((2, 2)),
        dma((2, 1)),
        dma((2,)),
        dma((2,)),
        dma((2, 2)),
        dma((2, 2)),
        dma((2, 1)),
        dma((2,)),
        dma((2, 2)),
        dma((2, 2)),
        dma((2, 1)),
        dma((2,)),
        dma((4,)),
        dma((2, 2)),
        dma((2, 2)),
        dma((2, 1)),
        dma((1,)),
        dma((4,)),
        dma((2, 4)),
        dma((2, 3)),
        dma((2,)),
        dma((2,)),
        dma((n,)),
        dma((2, n - 1)),
    ]


def per_device(n, n_col, snapshots, rotations):
    rows, width = snapshots.shape
    block = width // n
    paired = n == 8 and block == LANE and rows % (CHUNKS * TILE) == 0
    bf16, f32 = jnp.bfloat16, jnp.float32
    anywhere = pl.BlockSpec(memory_space=pl.ANY)
    inside = pl.BlockSpec(memory_space=pltpu.VMEM)
    shapes = (
        jax.ShapeDtypeStruct((block, width), f32),
        jax.ShapeDtypeStruct((block, width), f32),
        jax.ShapeDtypeStruct((rows, width), bf16),
    )
    if paired:
        body = functools.partial(paired_kernel, n_col)
    else:
        body = functools.partial(general_kernel, n, n_col)
    results = pl.pallas_call(
        body,
        out_shape=tuple(pltpu.VMEM(shape.shape, shape.dtype) for shape in shapes),
        in_specs=[anywhere] * 2,
        out_specs=(inside if paired else anywhere,) * 3,
        scratch_shapes=(paired_scratch if paired else general_scratch)(n, rows, width),
        compiler_params=pltpu.CompilerParams(
            collective_id=0, has_side_effects=True, vmem_limit_bytes=44 * 1024 * 1024
        ),
    )(*(pltpu.with_memory_space_constraint(a, pltpu.HBM) for a in (snapshots, rotations)))
    return pl.pallas_call(
        finish,
        out_shape=shapes,
        in_specs=[anywhere] * 3,
        out_specs=(anywhere,) * 3,
        scratch_shapes=[pltpu.SemaphoreType.DMA((3,))],
    )(*(pltpu.with_memory_space_constraint(r, pltpu.VMEM) for r in results))


def solution(mesh):
    return jax.shard_map(
        functools.partial(per_device, mesh.shape["row"], mesh.shape["col"]),
        mesh=mesh,
        in_specs=(P("row", "col"), P(None, "col", None)),
        out_specs=(P(("col", "row"), None), P(("col", "row"), None), P("row", "col")),
        check_vma=False,
    )
```

```python
import functools

import jax
import jax.numpy as jnp
from jax import lax
from jax.experimental import pallas as pl
from jax.experimental.pallas import tpu as pltpu
from jax.sharding import PartitionSpec as P

TILE = 256
LANE = 128
CHUNKS = 4


def paired_kernel(
    n_col, x_hbm, rot_hbm, g1, g2, out,
    x, rot, left, pair, moved, flip_x, flip_l, flip_r, strip,
    a_part, a_peer, a_sums, a_near, a_far, a_total, a_turn, a_turned,
    l_part, l_peer, l_sums, l_near, l_far, l_turn, l_turned, l_row, l_in,
    b_part, b_peer, b_sums, b_near, b_far, b_turn, b_turned,
    c_part, c_peer, c_sums, c_near, c_far, c_turn, c_turned,
    d_part, d_peer, d_sums, d_near, d_far, d_turn, d_turned,
    h_part, h_peer, h_sums, h_land, h_out, h_row, h_col,
    energy, energy_in,
    load_sem, left_send, left_recv, a_core, a_first, a_second, a_mirror,
    l_core, l_first, l_second, l_mirror, l_sem,
    b_core, b_first, b_second, b_mirror,
    c_core, c_first, c_second, c_mirror_send, c_mirror_recv,
    d_core, d_first, d_second, d_mirror_send, d_mirror_recv,
    h_core, h_z, h_send, h_row_recv, h_col_recv, e_sem,
):
    n = 8
    rows, width = x.shape
    half = width // 2
    scale = 1.0 / (rows * n)
    chunk = rows // CHUNKS
    f32, bf16 = jnp.float32, jnp.bfloat16

    me_col = lax.axis_index("col")
    me = lax.axis_index("row")
    core = lax.rem(me, 2)
    z = lax.div(me, 2)
    partner = me + 1 - 2 * core
    beside = z + 1 - 2 * lax.rem(z, 2)
    across = 3 - z
    opposite = lax.rem(z + 2, 4)
    following = lax.rem(me_col + 1, n_col)
    preceding = lax.rem(me_col + n_col - 1, n_col)

    def rows_of(q):
        return pl.ds(q * chunk, chunk)

    def load(source, target, at):
        return pltpu.make_async_copy(source, target, load_sem.at[at])

    load_x = [load(x_hbm.at[rows_of(q)], x.at[rows_of(q)], q) for q in range(CHUNKS)]
    parts = ((0, 0, TILE), (0, TILE, TILE), (0, half, half), (1, 0, width))
    load_r = [
        load(
            rot_hbm.at[s, :, pl.ds(first, size)], rot.at[s, :, pl.ds(first, size)], CHUNKS + k
        )
        for k, (s, first, size) in enumerate(parts)
    ]
    load_x[0].start()
    load_r[0].start()
    for q in range(1, CHUNKS):
        load_x[q].start()
    for k in range(1, 4):
        load_r[k].start()

    barrier = pltpu.get_barrier_semaphore()
    for other in (following, preceding):
        pl.semaphore_signal(
            barrier, inc=1, device_id={"col": other, "row": me},
            device_id_type=pl.DeviceIdType.MESH,
        )
    for step in range(1, n):
        pl.semaphore_signal(
            barrier, inc=1, device_id={"col": me_col, "row": lax.rem(me + step, n)},
            device_id_type=pl.DeviceIdType.MESH,
        )

    def remote(src, dst, send_sem, recv_sem, col, row):
        return pltpu.make_async_remote_copy(
            src_ref=src, dst_ref=dst, send_sem=send_sem, recv_sem=recv_sem,
            device_id={"col": col, "row": row}, device_id_type=pl.DeviceIdType.MESH,
        )

    def to_chip(src, dst, sems, at, chip):
        return remote(src, dst, sems.at[0, at], sems.at[1, at], me_col, 2 * chip + core)

    def mul(a, b):
        return jnp.dot(a, b, preferred_element_type=f32)

    def when(condition, run):
        if condition is True:
            run()
        else:
            pl.when(condition)(run)

    def left_copy(k):
        q = k % CHUNKS
        first, size = ((0, TILE), (TILE, LANE), (TILE + LANE, LANE))[k // CHUNKS]
        here = (rows_of(q), pl.ds(first, size))
        return remote(
            left.at[here], pair.at[here], left_send.at[k], left_recv.at[k], following, me
        )

    load_r[0].wait()
    for q in range(CHUNKS):
        load_x[q].wait()
        left[rows_of(q), 0:TILE] = mul(x[rows_of(q), :], rot[0, :, 0:TILE]).astype(bf16)
        if q == 0:
            pl.semaphore_wait(barrier, n + 1)
        left_copy(q).start()

    def core_copy(part, peer, sems, at):
        return remote(
            part.at[1 - core, at], peer.at[at], sems.at[0, at], sems.at[1, at], me_col, partner
        )

    def added(part, peer, at, span):
        return part[core, at, span, :].astype(f32) + peer[at, span, :].astype(f32)

    class Fly:
        def __init__(self, part, peer, sums, near, far, near_sems, far_sems, base, span, first, second,
                     shift=0, live=lambda d: True):
            self.part, self.peer, self.sums, self.near, self.far = part, peer, sums, near, far
            self.near_sems, self.far_sems, self.base, self.span = near_sems, far_sems, base, span
            self.first, self.second, self.shift, self.live = first, second, shift, live

        def near_copy(self, slot, d):
            return to_chip(
                self.sums.at[d - self.shift, self.span], self.near.at[slot, self.span],
                self.near_sems, 2 * self.base + slot, self.first,
            )

        def far_copy(self):
            return to_chip(
                self.sums.at[self.second - self.shift, self.span], self.far.at[self.span],
                self.far_sems, self.base, self.second,
            )

        def term(self, d):
            return added(self.part, self.peer, d - self.shift, self.span)

        def send_near(self):
            for slot, d in enumerate((self.first, opposite)):
                def run(slot=slot, d=d):
                    self.sums[d - self.shift, self.span, :] = self.term(d).astype(bf16)
                    self.near_copy(slot, d).start()
                when(self.live(d), run)

        def send_far(self):
            def run():
                d = self.second
                self.near_copy(1, d).wait_recv()
                self.sums[d - self.shift, self.span, :] = (
                    self.term(d) + self.near[1, self.span, :].astype(f32)
                ).astype(bf16)
                self.far_copy().start()
            when(self.live(self.second), run)

        def total(self):
            self.near_copy(0, z).wait_recv()
            to_chip(
                self.sums.at[z - self.shift, self.span], self.far.at[self.span],
                self.far_sems, self.base, self.second,
            ).wait_recv()
            return (
                self.term(z) + self.near[0, self.span, :].astype(f32)
                + self.far[self.span, :].astype(f32)
            ) * scale

        def drain(self):
            for slot, d in enumerate((self.first, opposite)):
                when(self.live(d), lambda slot=slot, d=d: self.near_copy(slot, d).wait_send())
            when(self.live(self.second), lambda: self.far_copy().wait_send())

    everything = pl.ds(0, LANE)
    upper, lower = pl.ds(0, LANE // 2), pl.ds(LANE // 2, LANE // 2)
    a_sum = (
        Fly(a_part, a_peer, a_sums, a_near, a_far, a_first, a_second, 0, upper, beside, across),
        Fly(a_part, a_peer, a_sums, a_near, a_far, a_first, a_second, 1, lower, beside, across),
    )
    b_sum = Fly(
        b_part, b_peer, b_sums, b_near, b_far, b_first, b_second, 0, everything, beside, across,
        shift=2, live=lambda d: d >= 2,
    )

    class Direct:
        def __init__(self, part, peer, sums, land, sems):
            self.part, self.peer, self.sums, self.land, self.sems = part, peer, sums, land, sems

        def copy(self, slot, source, chip):
            return to_chip(self.sums.at[source], self.land.at[slot], self.sems, slot, chip)

        def send(self):
            for slot, d in enumerate((opposite, across, beside)):
                self.sums[d] = added(self.part, self.peer, d, slice(None)).astype(bf16)
                self.copy(slot, d, d).start()

        def total(self):
            value = added(self.part, self.peer, z, slice(None))
            for slot, d in ((2, beside), (1, across), (0, opposite)):
                self.copy(slot, z, d).wait_recv()
                value = value + self.land[slot].astype(f32)
            return value * scale

        def drain(self):
            for slot, d in enumerate((opposite, across, beside)):
                self.copy(slot, d, d).wait_send()

    l_sum = Fly(
        l_part, l_peer, l_sums, l_near, l_far, l_first, l_second, 0, everything, beside, across,
        live=lambda d: d < 2,
    )
    c_sum = Fly(
        c_part, c_peer, c_sums, c_near, c_far, c_first, c_second, 0, everything, beside, across,
        shift=2, live=lambda d: d >= 2,
    )
    d_sum = Fly(
        d_part, d_peer, d_sums, d_near, d_far, d_first, d_second, 0, everything, beside, across,
        shift=2, live=lambda d: d >= 2,
    )
    h_sum = Direct(h_part, h_peer, h_sums, h_land, h_z)

    def column(block):
        if isinstance(block, int):
            return pl.ds(block * LANE, LANE)
        return pl.ds(pl.multiple_of(block * LANE, LANE), LANE)

    for d in range(4):
        flip_x[d] = x[:, d * TILE:(d + 1) * TILE].T
        for k in range(3):
            m = (d + k) % 4
            term = mul(flip_x[d], x[:, m * TILE:(m + 1) * TILE]).astype(bf16)
            for e in range(2):
                for b in range(2):
                    slot = 2 * k + b - e
                    if 0 <= slot <= 4:
                        a_part[e, d, :, slot * LANE:(slot + 1) * LANE] = term[
                            e * LANE:(e + 1) * LANE, b * LANE:(b + 1) * LANE
                        ]
        core_copy(a_part, a_peer, a_core, d).start()

    load_r[1].wait()
    for q in range(CHUNKS):
        left[rows_of(q), TILE:half] = mul(x[rows_of(q), :], rot[0, :, TILE:half]).astype(bf16)
        left_copy(CHUNKS + q).start()
    for q in range(CHUNKS):
        left_copy(2 * CHUNKS + q).start()

    for d in range(4):
        core_copy(a_part, a_peer, a_core, d).wait_recv()
    a_sum[0].send_near()
    def core_send(part, peer, sems, count):
        for d in range(count):
            core_copy(part, peer, sems, d).start()

    def core_wait(part, peer, sems, count):
        for d in range(count):
            core_copy(part, peer, sems, d).wait_recv()

    def ring_terms(source, first, flip, part, peer, sems):
        for d in range(2):
            flip[d * TILE:(d + 1) * TILE, :] = source[
                :, first + d * TILE:first + (d + 1) * TILE
            ].T
            term = mul(flip[d * TILE:(d + 1) * TILE, :], source[:, first:first + half]).astype(bf16)
            for e in range(2):
                for k in range(3):
                    at = (2 * d + e + k) % 4 * LANE
                    part[e, d, :, k * LANE:(k + 1) * LANE] = term[
                        e * LANE:(e + 1) * LANE, at:at + LANE
                    ]
            core_copy(part, peer, sems, d).start()

    ring_terms(left, 0, flip_l, l_part, l_peer, l_core)
    load_r[2].wait()

    def turn_right(first):
        def body(t, _):
            span = pl.ds(pl.multiple_of(t * TILE, TILE), TILE)
            pair[span, first:first + TILE] = mul(
                x[span, :], rot[0, :, first:first + TILE]
            ).astype(bf16)
            return 0
        lax.fori_loop(0, rows // TILE, body, 0)

    turn_right(half)
    core_wait(l_part, l_peer, l_core, 2)
    l_sum.send_near()
    a_sum[1].send_near()
    turn_right(half + TILE)

    ring_terms(pair, half, flip_r, b_part, b_peer, b_core)
    load_r[3].wait()

    def move_right(t, _):
        span = pl.ds(pl.multiple_of(t * TILE, TILE), TILE)
        moved[span, :] = mul(pair[span, half:], rot[1, half:, :])
        return 0

    lax.fori_loop(0, rows // TILE // 2, move_right, 0)
    a_sum[0].send_far()
    core_wait(b_part, b_peer, b_core, 2)
    b_sum.send_near()
    lax.fori_loop(rows // TILE // 2, rows // TILE, move_right, 0)
    a_sum[1].send_far()

    def move_left(t, _):
        span = pl.ds(pl.multiple_of(t * TILE, TILE), TILE)
        moved[span, :] += mul(pair[span, 0:TILE], rot[1, 0:TILE, :])
        return 0

    for q in range(CHUNKS):
        left_copy(q).wait_recv()
    for d in range(2):
        term = mul(flip_r[d * TILE:(d + 1) * TILE, :], pair[:, 0:TILE]).astype(bf16)
        c_part[0, d] = term[:LANE]
        c_part[1, d] = term[LANE:]
        core_copy(c_part, c_peer, c_core, d).start()
    lax.fori_loop(0, rows // TILE, move_left, 0)
    core_wait(c_part, c_peer, c_core, 2)
    l_sum.send_far()
    b_sum.send_far()
    c_sum.send_near()

    for q in range(CHUNKS):
        left_copy(CHUNKS + q).wait_recv()
    term = mul(flip_r[...], pair[:, column(2)]).astype(bf16)
    for i in range(4):
        d_part[i % 2, i // 2] = term[i * LANE:(i + 1) * LANE]
    core_send(d_part, d_peer, d_core, 2)

    edge = half // n

    def strip_rows(q):
        span = rows_of(q)
        left_copy(2 * CHUNKS + q).wait_recv()
        value = mul(flip_r[:, q * chunk:(q + 1) * chunk], pair[span, column(3)])
        if q > 0:
            value = value + strip[...]
        if q < CHUNKS - 1:
            strip[...] = value
        else:
            for i in range(n):
                h_part[i % 2, i // 2] = value[i * edge:(i + 1) * edge].astype(bf16)
            core_send(h_part, h_peer, h_core, 4)

    def move_rows(q):
        span = rows_of(q)
        value = moved[span, :] + mul(pair[span, TILE:half], rot[1, TILE:half, :])
        moved[span, :] = value
        return jnp.sum(value * value, axis=0, keepdims=True)

    strip_rows(0)
    squares = move_rows(0)
    core_wait(d_part, d_peer, d_core, 2)
    d_sum.send_near()

    def a_mirror_copy(k):
        return remote(
            a_turn.at[k - 1], a_turned.at[k - 1], a_mirror.at[0, k - 1], a_mirror.at[1, k - 1],
            me_col, lax.rem(me + k, n),
        )

    def l_mirror_copy():
        return remote(
            l_turn, l_turned, l_mirror.at[0], l_mirror.at[1], me_col, lax.rem(me + 1, 4)
        )

    def l_copy(col):
        return remote(l_row, l_in, l_sem.at[0], l_sem.at[1], col, me)

    def b_mirror_copy():
        return remote(
            b_turn, b_turned, b_mirror.at[0], b_mirror.at[1], me_col, 4 + lax.rem(me + 1, 4)
        )

    def c_mirror_copy(m, slot):
        return remote(
            c_turn.at[m], c_turned.at[slot], c_mirror_send.at[m], c_mirror_recv.at[slot],
            me_col, m,
        )

    def d_mirror_copy(slot):
        return remote(
            d_turn, d_turned.at[slot], d_mirror_send.at[0], d_mirror_recv.at[slot], me_col, 2
        )

    for q in range(1, CHUNKS - 1):
        strip_rows(q)
        squares = squares + move_rows(q)
    c_sum.send_far()
    d_sum.send_far()

    @pl.when(z < 2)
    def _():
        value = l_sum.total()
        l_turn[...] = value[:, LANE:2 * LANE].T.astype(bf16)
        l_mirror_copy().start()
        for k in range(3):
            l_row[:, column(lax.rem(me + k, 4))] = value[:, k * LANE:(k + 1) * LANE].astype(bf16)

    strip_rows(CHUNKS - 1)
    energy[...] = squares + move_rows(CHUNKS - 1)

    def e_copy(step):
        return remote(
            energy, energy_in.at[step - 1], e_sem.at[0, step - 1], e_sem.at[1, step - 1],
            me_col, lax.rem(me + step, n),
        )

    core_wait(h_part, h_peer, h_core, 4)
    h_sum.send()
    for step in range(1, n):
        e_copy(step).start()

    @pl.when(z < 2)
    def _():
        l_mirror_copy().wait_recv()
        l_row[:, column(lax.rem(me + 3, 4))] = l_turned[...]
        l_copy(following).start()

    for fly in a_sum:
        a_total[fly.span, :] = fly.total()
    for k in (3, 2, 1):
        a_turn[k - 1] = a_total[:, k * LANE:(k + 1) * LANE].T.astype(bf16)
        a_mirror_copy(k).start()
    for k in range(5):
        g1[:, column(lax.rem(me + k, n))] = a_total[:, k * LANE:(k + 1) * LANE]

    @pl.when(z >= 2)
    def _():
        value = b_sum.total()
        b_turn[...] = value[:, LANE:2 * LANE].T.astype(bf16)
        b_mirror_copy().start()
        for k in range(3):
            g2[:, column(4 + lax.rem(me + k, 4))] = value[:, k * LANE:(k + 1) * LANE]
        value = c_sum.total()
        g2[:, 0:TILE] = value
        for m in range(2):
            c_turn[m] = value[:, m * LANE:(m + 1) * LANE].T.astype(bf16)
            c_mirror_copy(m, me - 4).start()

    @pl.when(z >= 2)
    def _():
        value = d_sum.total()
        g2[:, column(2)] = value
        d_turn[...] = value.T.astype(bf16)
        d_mirror_copy(me - 4).start()


    total = energy[...]
    for step in range(1, n):
        e_copy(step).wait_recv()
        total = total + energy_in[step - 1]
    singular = jnp.sqrt(total * scale + 1e-06)
    factor = jnp.maximum(singular - 1.8, 0.0) / singular

    def shrink(t, _):
        span = pl.ds(pl.multiple_of(t * TILE, TILE), TILE)
        out[span, :] = (moved[span, :] * factor).astype(bf16)
        return 0

    lax.fori_loop(0, rows // TILE, shrink, 0)

    def h_row_copy(slot, row):
        return remote(h_out, h_row.at[slot], h_send.at[0], h_row_recv.at[slot], me_col, row)

    def h_col_copy(slot, row):
        place = slot * edge if isinstance(slot, int) else pl.multiple_of(slot * edge, edge)
        return remote(
            h_out, h_col.at[pl.ds(place, edge)], h_send.at[1], h_col_recv.at[slot], me_col, row
        )

    value = h_sum.total()
    h_out[...] = value.astype(bf16)

    @pl.when(me != 3)
    def _():
        h_col_copy(me, 3).start()

    @pl.when(me != 7)
    def _():
        h_row_copy(core, 4 + z).start()

    @pl.when(me == 3)
    def _():
        h_col[3 * edge:4 * edge, :] = value.astype(bf16)

    for k in (1, 2, 3):
        a_mirror_copy(k).wait_recv()
        g1[:, column(lax.rem(me + n - k, n))] = a_turned[k - 1].astype(f32)

    @pl.when(z >= 2)
    def _():
        b_mirror_copy().wait_recv()
        g2[:, column(4 + lax.rem(me + 3, 4))] = b_turned[...].astype(f32)

    @pl.when(z < 2)
    def _():
        l_copy(preceding).wait_recv()
        g2[:, 0:half] = l_in[...].astype(f32)

    @pl.when(z == 0)
    def _():
        for slot in range(4):
            remote(
                c_turn.at[0], c_turned.at[slot], c_mirror_send.at[0], c_mirror_recv.at[slot],
                me_col, partner,
            ).wait_recv()
            g2[:, column(4 + slot)] = c_turned[slot].astype(f32)

    @pl.when(me == 2)
    def _():
        for slot in range(4):
            remote(
                d_turn, d_turned.at[slot], d_mirror_send.at[0], d_mirror_recv.at[slot],
                me_col, partner,
            ).wait_recv()
            g2[:, column(4 + slot)] = d_turned[slot].astype(f32)

    @pl.when(z >= 2)
    def _():
        h_row_copy(0, partner).wait_recv()
        g2[0:edge, column(3)] = h_row[0].astype(f32)

    @pl.when((z >= 2) & (me != 7))
    def _():
        h_row_copy(1, partner).wait_recv()
        g2[edge:2 * edge, column(3)] = h_row[1].astype(f32)

    @pl.when(me == 7)
    def _():
        g2[edge:2 * edge, column(3)] = value

    @pl.when(me == 3)
    def _():
        for slot in range(n):
            if slot != 3:
                h_col_copy(slot, partner).wait_recv()
        for block in range(4):
            g2[:, column(4 + block)] = h_col[block * LANE:(block + 1) * LANE, :].T.astype(f32)

    for k in range(3 * CHUNKS):
        left_copy(k).wait_send()
    for part, peer, sems, count in (
        (a_part, a_peer, a_core, 4), (l_part, l_peer, l_core, 2), (b_part, b_peer, b_core, 2),
        (c_part, c_peer, c_core, 2), (d_part, d_peer, d_core, 2), (h_part, h_peer, h_core, 4),
    ):
        for d in range(count):
            core_copy(part, peer, sems, d).wait_send()
    for flow in (*a_sum, l_sum, b_sum, c_sum, d_sum, h_sum):
        flow.drain()
    for k in (1, 2, 3):
        a_mirror_copy(k).wait_send()

    @pl.when(z < 2)
    def _():
        l_mirror_copy().wait_send()
        l_copy(following).wait_send()

    @pl.when(z >= 2)
    def _():
        b_mirror_copy().wait_send()
        for m in range(2):
            c_mirror_copy(m, me - 4).wait_send()
        d_mirror_copy(me - 4).wait_send()

    @pl.when(me != 3)
    def _():
        h_col_copy(me, 3).wait_send()

    @pl.when(me != 7)
    def _():
        h_row_copy(core, 4 + z).wait_send()

    for step in range(1, n):
        e_copy(step).wait_send()


def general_kernel(
    n, n_col, x_hbm, rot_hbm, g1_hbm, g2_hbm, out_hbm,
    x, rot, left, pair, moved, part, peer, sums, landed,
    gram_out, energy, energy_in, shrunk,
    load_sem, left_send, left_recv, core_send, core_recv, z_send, z_recv,
    e_send, e_recv, store_sem, shrunk_sem,
):
    rows, width = x.shape
    half = width // 2
    block = width // n
    groups = n // 2
    total_rows = rows * n
    tiles = width // TILE
    row_tiles = rows // TILE
    per_tile = TILE // (2 * block)

    me_col = lax.axis_index("col")
    me = lax.axis_index("row")
    core = lax.rem(me, 2)
    group = lax.div(me, 2)
    partner = me + 1 - 2 * core

    def peer_at(step):
        return lax.rem(me + step, n)

    load_x = pltpu.make_async_copy(x_hbm, x, load_sem.at[0])
    load_r0 = [
        pltpu.make_async_copy(
            rot_hbm.at[0, :, pl.ds(h * half, half)], rot.at[0, :, pl.ds(h * half, half)],
            load_sem.at[1 + h],
        )
        for h in range(2)
    ]
    load_r1 = pltpu.make_async_copy(rot_hbm.at[1], rot.at[1], load_sem.at[3])
    load_x.start()
    load_r0[0].start()
    load_r0[1].start()
    load_r1.start()

    following = lax.rem(me_col + 1, n_col)
    preceding = lax.rem(me_col + n_col - 1, n_col)
    barrier = pltpu.get_barrier_semaphore()
    for other in (following, preceding):
        pl.semaphore_signal(
            barrier, inc=1, device_id={"col": other, "row": me},
            device_id_type=pl.DeviceIdType.MESH,
        )
    for step in range(1, n):
        pl.semaphore_signal(
            barrier, inc=1, device_id={"col": me_col, "row": peer_at(step)},
            device_id_type=pl.DeviceIdType.MESH,
        )

    def remote(src, dst, send_sem, recv_sem, col, row):
        return pltpu.make_async_remote_copy(
            src_ref=src, dst_ref=dst, send_sem=send_sem, recv_sem=recv_sem,
            device_id={"col": col, "row": row}, device_id_type=pl.DeviceIdType.MESH,
        )

    def turn(into, first, column):
        def body(t, _):
            span = pl.ds(pl.multiple_of(t * TILE, TILE), TILE)
            into[span, pl.ds(column - first, TILE)] = jnp.dot(
                x[span, :], rot[0, :, pl.ds(column, TILE)], preferred_element_type=jnp.float32
            ).astype(jnp.bfloat16)
            return 0
        lax.fori_loop(0, row_tiles, body, 0)

    pieces = half // TILE
    left_copy = [
        remote(
            left.at[:, pl.ds(h * TILE, TILE)], pair.at[:, pl.ds(h * TILE, TILE)],
            left_send.at[h], left_recv.at[h], following, me,
        )
        for h in range(pieces)
    ]
    load_x.wait()
    load_r0[0].wait()
    turn(left, 0, 0)
    pl.semaphore_wait(barrier, n + 1)
    left_copy[0].start()

    def z_copy(s, u):
        g = lax.rem(group + u, groups)
        k = lax.rem(g - group + 2 * groups - 1, groups)
        return remote(
            sums.at[s, g], landed.at[s, 0, k], z_send.at[s, k], z_recv.at[s, 0, k],
            me_col, 2 * g + core,
        )

    def added(s, u):
        return part[s, core, u].astype(jnp.float32) + peer[s, u].astype(jnp.float32)

    def rows_copy(s, q):
        span = pl.ds(q * per_tile, per_tile)
        return remote(
            part.at[s, 1 - core, span], peer.at[s, span],
            core_send.at[s, q], core_recv.at[s, q], me_col, partner,
        )

    def rows_terms(s, source):
        def body(q, _):
            turned_tile = source[:, pl.ds(pl.multiple_of(q * TILE, TILE), TILE)].T
            for m in range(tiles):
                term = jnp.dot(
                    turned_tile, source[:, m * TILE:(m + 1) * TILE],
                    preferred_element_type=jnp.float32,
                ).astype(jnp.bfloat16)
                for e in range(2 * per_tile):
                    part[s, e % 2, q * per_tile + e // 2, :, m * TILE:(m + 1) * TILE] = term[
                        e * block:(e + 1) * block, :
                    ]
            rows_copy(s, q).start()
            return 0
        lax.fori_loop(0, tiles, body, 0)

    def rows_pass(s):
        for q in range(tiles):
            rows_copy(s, q).wait_recv()

        def body(k, _):
            g = lax.rem(group + k, groups)
            sums[s, g] = added(s, g).astype(jnp.bfloat16)
            z_copy(s, k).start()
            return 0
        lax.fori_loop(1, groups, body, 0)

    def rows_sum(s):
        total = added(s, group)
        for k in range(1, groups):
            z_copy(s, k).wait_recv()
            total = total + landed[s, 0, k - 1].astype(jnp.float32)
        gram_out[s] = total / total_rows

    def gram_store(s, target):
        return pltpu.make_async_copy(gram_out.at[s], target, store_sem.at[s])

    rows_terms(0, x)
    for h in range(1, pieces):
        turn(left, 0, h * TILE)
        left_copy[h].start()
    rows_pass(0)
    load_r0[1].wait()
    for h in range(pieces):
        turn(pair, 0, half + h * TILE)
    load_r1.wait()

    def add_moved(first, depth, fresh):
        def body(t, acc):
            span = pl.ds(pl.multiple_of(t * TILE, TILE), TILE)
            value = jnp.dot(
                pair[span, pl.ds(first, depth)], rot[1, pl.ds(first, depth), :],
                preferred_element_type=jnp.float32,
            )
            if not fresh:
                value = value + moved[span, :]
            moved[span, :] = value
            return acc + jnp.sum(value * value, axis=0, keepdims=True)
        return lax.fori_loop(0, row_tiles, body, jnp.zeros((1, width), jnp.float32))

    add_moved(half, half, True)
    left_copy[0].wait_recv()
    for h in range(pieces - 1):
        if h > 0:
            left_copy[h].wait_recv()
        add_moved(h * TILE, TILE, False)
    rows_sum(0)
    gram_store(0, g1_hbm).start()
    left_copy[pieces - 1].wait_recv()
    rows_terms(1, pair)
    energy[...] = add_moved(half - TILE, TILE, False)

    def e_copy(step):
        return remote(
            energy, energy_in.at[step - 1], e_send.at[step - 1], e_recv.at[step - 1],
            me_col, peer_at(step),
        )

    rows_pass(1)
    total = energy[...]
    for step in range(1, n):
        e_copy(step).wait_recv()
        total = total + energy_in[step - 1]
    singular = jnp.sqrt(total / total_rows + 1e-06)
    factor = jnp.maximum(singular - 1.8, 0.0) / singular

    def out_copy(t):
        span = pl.ds(pl.multiple_of(t * TILE, TILE), TILE)
        return pltpu.make_async_copy(shrunk.at[span, :], out_hbm.at[span, :], shrunk_sem.at[t])

    def shrink(t, _):
        span = pl.ds(pl.multiple_of(t * TILE, TILE), TILE)
        shrunk[span, :] = (moved[span, :] * factor).astype(jnp.bfloat16)
        out_copy(t).start()
        return 0

    lax.fori_loop(0, row_tiles, shrink, 0)
    rows_sum(1)
    gram_store(1, g2_hbm).start()

    for h in range(pieces):
        left_copy[h].wait_send()
    for s in range(2):
        for q in range(tiles):
            rows_copy(s, q).wait_send()
        for k in range(1, groups):
            z_copy(s, k).wait_send()
    for step in range(1, n):
        e_copy(step).wait_send()
    for t in range(row_tiles):
        out_copy(t).wait()
    gram_store(0, g1_hbm).wait()
    gram_store(1, g2_hbm).wait()


def finish(*refs):
    sources, targets, sem = refs[:3], refs[3:6], refs[6]
    stores = [
        pltpu.make_async_copy(source, target, sem.at[at])
        for at, (source, target) in enumerate(zip(sources, targets))
    ]
    for store in reversed(stores):
        store.start()
    for store in stores:
        store.wait()


def general_scratch(n, rows, width):
    half = width // 2
    block = width // n
    groups = n // 2
    tiles = width // TILE
    sends = max(groups - 1, tiles)
    bf16, f32, dma = jnp.bfloat16, jnp.float32, pltpu.SemaphoreType.DMA
    return [
        pltpu.VMEM((rows, width), bf16),
        pltpu.VMEM((2, width, width), bf16),
        pltpu.VMEM((rows, half), bf16),
        pltpu.VMEM((rows, width), bf16),
        pltpu.VMEM((rows, width), f32),
        pltpu.VMEM((2, 2, groups, block, width), bf16),
        pltpu.VMEM((2, groups, block, width), bf16),
        pltpu.VMEM((2, groups, block, width), bf16),
        pltpu.VMEM((2, 1, groups - 1, block, width), bf16),
        pltpu.VMEM((2, block, width), f32),
        pltpu.VMEM((1, width), f32),
        pltpu.VMEM((n - 1, 1, width), f32),
        pltpu.VMEM((rows, width), bf16),
        dma((4,)),
        dma((half // TILE,)),
        dma((half // TILE,)),
        dma((2, sends)),
        dma((2, sends)),
        dma((2, sends)),
        dma((2, 1, groups - 1)),
        dma((n - 1,)),
        dma((n - 1,)),
        dma((2,)),
        dma((rows // TILE,)),
    ]


def paired_scratch(n, rows, width):
    half = width // 2
    bf16, f32, dma = jnp.bfloat16, jnp.float32, pltpu.SemaphoreType.DMA

    def room(*shape):
        return pltpu.VMEM(shape, bf16)

    return [
        room(rows, width),
        room(2, width, width),
        room(rows, half),
        room(rows, width),
        pltpu.VMEM((rows, width), f32),
        room(4, TILE, rows),
        room(half, rows),
        room(half, rows),
        pltpu.VMEM((half, LANE), f32),
        room(2, 4, LANE, 5 * LANE),
        room(4, LANE, 5 * LANE),
        room(4, LANE, 5 * LANE),
        room(2, LANE, 5 * LANE),
        room(LANE, 5 * LANE),
        pltpu.VMEM((LANE, 5 * LANE), f32),
        room(3, LANE, LANE),
        room(3, LANE, LANE),
        room(2, 2, LANE, 3 * LANE),
        room(2, LANE, 3 * LANE),
        room(2, LANE, 3 * LANE),
        room(2, LANE, 3 * LANE),
        room(LANE, 3 * LANE),
        room(LANE, LANE),
        room(LANE, LANE),
        room(LANE, half),
        room(LANE, half),
        room(2, 2, LANE, 3 * LANE),
        room(2, LANE, 3 * LANE),
        room(2, LANE, 3 * LANE),
        room(2, LANE, 3 * LANE),
        room(LANE, 3 * LANE),
        room(LANE, LANE),
        room(LANE, LANE),
        room(2, 2, LANE, TILE),
        room(2, LANE, TILE),
        room(2, LANE, TILE),
        room(2, LANE, TILE),
        room(LANE, TILE),
        room(2, LANE, LANE),
        room(4, LANE, LANE),
        room(2, 2, LANE, LANE),
        room(2, LANE, LANE),
        room(2, LANE, LANE),
        room(2, LANE, LANE),
        room(LANE, LANE),
        room(LANE, LANE),
        room(4, LANE, LANE),
        room(2, 4, half // n, LANE),
        room(4, half // n, LANE),
        room(4, half // n, LANE),
        room(3, half // n, LANE),
        room(half // n, LANE),
        room(2, half // n, LANE),
        room(half, LANE),
        pltpu.VMEM((1, width), f32),
        pltpu.VMEM((n - 1, 1, width), f32),
        dma((CHUNKS + 4,)),
        dma((3 * CHUNKS,)),
        dma((3 * CHUNKS,)),
        dma((2, 4)),
        dma((2, 4)),
        dma((2, 2)),
        dma((2, 3)),
        dma((2, 2)),
        dma((2, 2)),
        dma((2, 1)),
        dma((2,)),
        dma((2,)),
        dma((2, 2)),
        dma((2, 2)),
        dma((2, 1)),
        dma((2,)),
        dma((2, 2)),
        dma((2, 2)),
        dma((2, 1)),
        dma((2,)),
        dma((4,)),
        dma((2, 2)),
        dma((2, 2)),
        dma((2, 1)),
        dma((1,)),
        dma((4,)),
        dma((2, 4)),
        dma((2, 3)),
        dma((2,)),
        dma((2,)),
        dma((n,)),
        dma((2, n - 1)),
    ]


def per_device(n, n_col, snapshots, rotations):
    rows, width = snapshots.shape
    block = width // n
    paired = n == 8 and block == LANE and rows % (CHUNKS * TILE) == 0
    bf16, f32 = jnp.bfloat16, jnp.float32
    anywhere = pl.BlockSpec(memory_space=pl.ANY)
    inside = pl.BlockSpec(memory_space=pltpu.VMEM)
    shapes = (
        jax.ShapeDtypeStruct((block, width), f32),
        jax.ShapeDtypeStruct((block, width), f32),
        jax.ShapeDtypeStruct((rows, width), bf16),
    )
    if paired:
        body = functools.partial(paired_kernel, n_col)
    else:
        body = functools.partial(general_kernel, n, n_col)
    results = pl.pallas_call(
        body,
        out_shape=tuple(pltpu.VMEM(shape.shape, shape.dtype) for shape in shapes),
        in_specs=[anywhere] * 2,
        out_specs=(inside if paired else anywhere,) * 3,
        scratch_shapes=(paired_scratch if paired else general_scratch)(n, rows, width),
        compiler_params=pltpu.CompilerParams(
            collective_id=0, has_side_effects=True, vmem_limit_bytes=44 * 1024 * 1024
        ),
    )(*(pltpu.with_memory_space_constraint(a, pltpu.HBM) for a in (snapshots, rotations)))
    return pl.pallas_call(
        finish,
        out_shape=shapes,
        in_specs=[anywhere] * 3,
        out_specs=(anywhere,) * 3,
        scratch_shapes=[pltpu.SemaphoreType.DMA((3,))],
    )(*(pltpu.with_memory_space_constraint(r, pltpu.VMEM) for r in results))


def solution(mesh):
    return jax.shard_map(
        functools.partial(per_device, mesh.shape["row"], mesh.shape["col"]),
        mesh=mesh,
        in_specs=(P("row", "col"), P(None, "col", None)),
        out_specs=(P(("col", "row"), None), P(("col", "row"), None), P("row", "col")),
        check_vma=False,
    )
```
